128 devices in a mesh: dp: 4 (over y), band: 32 (over x, z, core).
Axes of the slice: x: 4, y: 4, z: 4, core: 2. Of those that a mesh axis runs over, the one named last changes fastest.
Arguments:
- features: bfloat16 [4, 256, 5504], P('dp', None, 'band'), may hold values from -6 to 6
- corner_rows: int32 [4, 8, 64, 5504], P('dp', None, None, 'band'), may hold values from 0 to 5503, as said below
- corner_weights: float32 [4, 8, 64, 5504], P('dp', None, None, 'band'), may hold values from 0 to 1, as said below
- out_grad: bfloat16 [4, 256, 5504], P('dp', None, 'band'), may hold values from -6 to 6
- value_weight: bfloat16 [256, 256], replicated, may hold values from -0.375 to 0.375
- logit_weight: bfloat16 [256, 128], replicated, may hold values from -0.375 to 0.375
- output_weight: bfloat16 [256, 256], replicated, may hold values from -0.375 to 0.375
Outputs:
- input_grad: bfloat16 [4, 256, 5504], P('dp', None, 'band')
- value_weight_grad: float32 [256, 256], replicated
- logit_weight_grad: float32 [256, 128], replicated
- output_weight_grad: float32 [256, 256], replicated
The draws below stay inside these ranges and needn't reach their ends.
Inputs may be any that keep to these rules, and one draw needn't show every extreme that they name: `corner_rows`: cells are numbered band by band: cell t belongs to band t // 172; in a band's block the first 128 cells are of level 0, then 128 // 4 of level 1, 8 of level 2, 4 of level 3. An entry with k // 16 = l names a cell of level l. Every entry of a query in band b names a cell of band b - 1, b or b + 1. `corner_weights`: each group of four corners holds (1 - a)(1 - b), (1 - a) b, a (1 - b), a b for some a and b in [0, 1), so the four sum to one.
All inputs are finite; a program needn't handle non-finite values.
Results may differ from the reference program's by a relative error of at most 0.0064.
Values may be sent and summed in bfloat16 or wider, within the bound.
A program may use at most 64 MiB of HBM per device.

```python
import math
import jax
import jax.numpy as jnp
from jax import lax

D = 256
HEADS = 8
LEVELS = 4
POINTS = 4
TOK_DEV = 128
NT = 5504
IMAGES = 4


def draw_corner_rows(key, part):
    band_cells = TOK_DEV * 43 // 32
    band_total = NT // band_cells
    columns = jnp.arange(NT, dtype=jnp.int32)
    owner_band = columns // band_cells
    level_cells = [TOK_DEV, TOK_DEV // 4, TOK_DEV // 16, TOK_DEV // 32]
    level_width = [TOK_DEV // 4, TOK_DEV // 8, TOK_DEV // 16, TOK_DEV // 32]
    level_start = [0, TOK_DEV, TOK_DEV + TOK_DEV // 4, TOK_DEV + TOK_DEV // 4 + TOK_DEV // 16]
    shape = (IMAGES, HEADS, POINTS, NT)
    stacked = []
    for level in range(4):
        cells = level_cells[level]
        width = level_width[level]
        per_band = cells // width
        total_lines = band_total * per_band
        lower = jnp.maximum((owner_band - 1) * per_band, 0)
        upper = jnp.minimum((owner_band + 2) * per_band - 1, total_lines - 1)
        line = jax.random.randint(jax.random.fold_in(key, 17 + level), shape, lower, upper, dtype=jnp.int32)
        across = jax.random.randint(jax.random.fold_in(key, 41 + level), shape, 0, width - 1, dtype=jnp.int32)
        corner = line * width + across
        corners = jnp.stack([corner, corner + 1, corner + width, corner + width + 1], axis=3)
        flat = corners // cells * band_cells + level_start[level] + corners % cells
        stacked.append(flat)
    joined = jnp.stack(stacked, axis=2)
    return joined.reshape(IMAGES, HEADS, LEVELS * POINTS * 4, NT).astype(jnp.int32)


def draw_corner_weights(key, part):
    fractions = jax.random.uniform(jax.random.fold_in(key, 91), (IMAGES, HEADS, LEVELS * POINTS, 2, NT), jnp.float32)
    down = fractions[:, :, :, 0]
    across = fractions[:, :, :, 1]
    weights = jnp.stack([(1.0 - down) * (1.0 - across), (1.0 - down) * across, down * (1.0 - across), down * across], axis=3)
    return weights.reshape(IMAGES, HEADS, LEVELS * POINTS * 4, NT).astype(jnp.float32)


def level_of(stream_key, shape, split, low, largest):
    loudness = 1.0
    for axis_at, shards_of in split:
        draws = jax.random.uniform(jax.random.fold_in(jax.random.fold_in(stream_key, 6), axis_at), (shards_of,), jnp.float32, low / len(split), largest / len(split))
        loudness = loudness * jnp.repeat(jnp.exp(draws), shape[axis_at] // shards_of).reshape((-1,) + (1,) * (len(shape) - 1 - axis_at))
    return loudness


def normal_values(rng, dims, scale, most, shards=(), kind=jnp.bfloat16):
    factor_of = level_of(rng, dims, shards, -0.22, 0.18) if shards else 1.0
    drawn = jax.random.normal(rng, dims, jnp.float32) * scale * factor_of
    return jnp.minimum(jnp.maximum(drawn, -most), most).astype(kind)


def setup_inputs(seed: int = 0) -> dict:
    key_list = jax.random.split(jax.random.key(seed), 8)
    return {
        "features": normal_values(key_list[0], (IMAGES, D, NT), 1.0, 6.0, ((0, 4), (2, 32))),
        "corner_rows": draw_corner_rows(jax.random.fold_in(key_list[7], 71), 0),
        "corner_weights": draw_corner_weights(jax.random.fold_in(key_list[7], 71), 0),
        "out_grad": normal_values(key_list[3], (IMAGES, D, NT), 1.0, 6.0, ((0, 4), (2, 32))),
        "value_weight": normal_values(key_list[4], (D, D), D ** -0.5, 0.375),
        "logit_weight": normal_values(key_list[5], (D, HEADS * LEVELS * POINTS), D ** -0.5, 0.375),
        "output_weight": normal_values(key_list[6], (D, D), D ** -0.5, 0.375),
    }


def contract(left, right):
    return lax.dot_general(left, right, (((1,), (1,)), ((), ())), preferred_element_type=jnp.float32)

def head_pass(inputs):
    lookup_head, rows_head, blend_head, bilinear, grad_head = inputs
    picked = jnp.take(lookup_head, rows_head, axis=1).astype(jnp.float32)
    blend_wide = blend_head.astype(jnp.float32)
    grad_wide = grad_head.astype(jnp.float32)
    sampled = jnp.einsum('ekq,kq->eq', picked, blend_wide, precision=lax.Precision.HIGHEST)
    blend_grad = jnp.einsum('ekq,eq->kq', picked, grad_wide, precision=lax.Precision.HIGHEST)
    attn_grad = lax.optimization_barrier(jnp.sum((blend_grad * bilinear).reshape(-1, 4, bilinear.shape[1]), axis=1))
    contribution = blend_wide[None, :, :] * grad_wide[:, None, :]
    partial_value = jnp.zeros((lookup_head.shape[0], lookup_head.shape[1]), jnp.float32)
    partial_value = partial_value.at[:, rows_head].add(contribution)
    return (sampled, attn_grad, partial_value)

def reference(features, corner_rows, corner_weights, out_grad, value_weight, logit_weight, output_weight):
    head_count = HEADS
    head_size = D // HEADS
    points_all = LEVELS * POINTS
    grad_value_w = jnp.zeros((D, D), jnp.float32)
    grad_logit_w = jnp.zeros((D, head_count * points_all), jnp.float32)
    grad_output_w = jnp.zeros((D, D), jnp.float32)
    results = []
    for picture in range(IMAGES):
        inputs = features[picture]
        values_map = jnp.dot(value_weight.T, inputs, preferred_element_type=jnp.float32).astype(jnp.bfloat16)
        logits = jnp.dot(logit_weight.T, inputs, preferred_element_type=jnp.float32).reshape(head_count, points_all, -1)
        exponent = jnp.exp(logits)
        attention = exponent / lax.optimization_barrier(jnp.sum(exponent, axis=1, keepdims=True))
        blend = (jnp.repeat(attention, 4, axis=1) * corner_weights[picture]).astype(jnp.bfloat16)
        sample_grad = jnp.dot(output_weight, out_grad[picture], preferred_element_type=jnp.float32).astype(jnp.bfloat16)
        sampled, attn_grad, partial_value = lax.map(head_pass, (values_map.reshape(head_count, head_size, -1), corner_rows[picture], blend, corner_weights[picture], sample_grad.reshape(head_count, head_size, -1)))
        sampled = sampled.reshape(D, -1).astype(jnp.bfloat16)
        value_grad = partial_value.reshape(D, -1).astype(jnp.bfloat16)
        logit_grad = attention * (attn_grad - lax.optimization_barrier(jnp.sum(attention * attn_grad, axis=1, keepdims=True)))
        logit_grad = logit_grad.reshape(head_count * points_all, -1).astype(jnp.bfloat16)
        grad_output_w = grad_output_w + contract(sampled, out_grad[picture])
        grad_logit_w = grad_logit_w + contract(inputs, logit_grad)
        grad_value_w = grad_value_w + contract(inputs, value_grad)
        input_grad = jnp.dot(value_weight, value_grad, preferred_element_type=jnp.float32) + jnp.dot(logit_weight, logit_grad, preferred_element_type=jnp.float32)
        results.append(input_grad.astype(jnp.bfloat16))
    norm_scale = 1.0 / math.sqrt(IMAGES * NT)
    return (jnp.stack(results), grad_value_w * norm_scale, grad_logit_w * norm_scale, grad_output_w * norm_scale)
```

```python
import functools

import jax
import jax.numpy as jnp
from jax import lax
from jax.experimental import pallas as pl
from jax.experimental.pallas import tpu as pltpu
from jax.sharding import PartitionSpec as P

HEADS = 8
LEVELS = 4
POINTS = 4
D = 256
CELLS = 172
PAD = 176
TAIL = CELLS - 128
GAP = 128 - 2 * TAIL
LANES = 384
HEAD = D // HEADS
PTS = LEVELS * POINTS
BF = jnp.bfloat16
F32 = jnp.float32


def dot(a, b, ca=1, cb=0):
    return lax.dot_general(a, b, (((ca,), (cb,)), ((), ())), preferred_element_type=F32)


def local_kernel(
    x_ref,
    rows_ref,
    cw_ref,
    og_ref,
    vw_ref,
    lw_ref,
    ow_ref,
    low_ref,
    own_ref,
    high_ref,
    lg_ref,
    gv_ref,
    gl_ref,
    go_ref,
    v_s,
    att_s,
    g_s,
    samp_s,
    rep_s,
    vg_s,
    wide_s,
    m_s,
):
    band = lax.axis_index("band")
    x = x_ref[1]
    og = og_ref[...]
    for j in range(3):
        v_s[j] = dot(vw_ref[...], x_ref[j], 0, 0).astype(BF)
    logits = dot(lw_ref[...], x, 0, 0)
    att_s[...] = logits.reshape(HEADS, PTS, CELLS)
    g_s[...] = dot(ow_ref[...], og).astype(BF).astype(F32)

    def packed(first, second, rows):
        tail = jnp.concatenate(
            [first[:, 128:], second[:, 128:], jnp.zeros((rows, GAP), first.dtype)], axis=1
        )
        return [first[:, :128], second[:, :128], tail]

    def pair(i, carry):
        h0 = 2 * i
        h1 = 2 * i + 1
        hs = pl.ds(pl.multiple_of(i * 2 * HEAD, 2 * HEAD), 2 * HEAD)
        base = (band - 1) * CELLS
        cells = packed(rows_ref[h0] - base, rows_ref[h1] - base, 64)
        cw = packed(cw_ref[h0], cw_ref[h1], 64)
        logit = packed(att_s[h0], att_s[h1], PTS)
        g0 = g_s[pl.ds(pl.multiple_of(i * 2 * HEAD, HEAD), HEAD), :]
        g1 = g_s[pl.ds(pl.multiple_of(i * 2 * HEAD + HEAD, HEAD), HEAD), :]
        none = jnp.zeros((HEAD, 128), F32)
        gap = jnp.zeros((HEAD, 128 - TAIL), F32)
        top = [g0[:, :128], none, jnp.concatenate([g0[:, 128:], gap], axis=1)]
        bottom = [
            none,
            g1[:, :128],
            jnp.concatenate([none[:, :TAIL], g1[:, 128:], none[:, : 128 - 2 * TAIL]], axis=1),
        ]
        att = []
        for g in range(3):
            e = jnp.exp(logit[g])
            att.append(e / jnp.sum(e, axis=0, keepdims=True))
            for c in range(4):
                rep_s[pl.ds(c, PTS, stride=4), :] = att[g]
            over1 = cells[g] >= CELLS
            over2 = cells[g] >= 2 * CELLS
            r = cells[g] - jnp.where(over2, 2 * CELLS, jnp.where(over1, CELLS, 0))
            w = (rep_s[...] * cw[g]).astype(BF).astype(F32)
            zero = jnp.zeros_like(w)
            ls = slice(g * 128, (g + 1) * 128)
            wide_s[0, :, ls] = r.astype(F32)
            wide_s[1, :, ls] = jnp.where(over1, zero, w)
            wide_s[2, :, ls] = jnp.where(jnp.logical_and(over1, jnp.logical_not(over2)), w, zero)
            wide_s[3, :, ls] = jnp.where(over2, w, zero)

        def wide(n, k):
            row = jnp.broadcast_to(wide_s[n, pl.ds(k, 1), :], (16, LANES))
            return row.astype(BF)

        sub = lax.broadcasted_iota(jnp.int32, (16, LANES), 0)
        for cb in range(11):
            if cb < 8:
                levels = (0,)
            elif cb < 10:
                levels = (1,)
            else:
                levels = (2, 3)
            ids = (sub + cb * 16).astype(F32).astype(BF)
            acc = [jnp.zeros((16, LANES), BF) for _ in range(3)]
            for lev in levels:
                for k in range(lev * 16, lev * 16 + 16):
                    hit = wide(0, k) == ids
                    for j in range(3):
                        acc[j] = acc[j] + jnp.where(hit, wide(1 + j, k), jnp.zeros((), BF))
            for j in range(3):
                m_s[j, cb * 16 : cb * 16 + 16, :] = acc[j]

        gp = jnp.concatenate(
            [jnp.concatenate(top, axis=1), jnp.concatenate(bottom, axis=1)], axis=0
        ).astype(BF)
        samp = jnp.zeros((2 * HEAD, LANES), F32)
        for j in range(3):
            m_j = m_s[j, :CELLS, :]
            samp = samp + dot(v_s[j, hs, :], m_j)
            vg_s[j, hs, :] = dot(gp, m_j, 1, 1).astype(BF)
        s0 = jnp.concatenate([samp[:HEAD, :128], samp[:HEAD, 256 : 256 + TAIL]], axis=1)
        s1 = jnp.concatenate(
            [samp[HEAD:, 128:256], samp[HEAD:, 256 + TAIL : 256 + 2 * TAIL]], axis=1
        )
        samp_s[hs, :] = jnp.concatenate([s0, s1], axis=0).astype(BF)

        lgs = []
        for g in range(3):
            at = jnp.concatenate([cells[g], jnp.zeros((64, 128), jnp.int32)], axis=0).T
            over1 = at >= CELLS
            over2 = at >= 2 * CELLS
            r = at - jnp.where(over2, 2 * CELLS, jnp.where(over1, CELLS, 0))
            first = jnp.clip(r, 0, 127)
            rest = jnp.clip(r - 128, 0, 127)
            g_t = jnp.concatenate([top[g], bottom[g]], axis=0).T.astype(BF)
            pick = jnp.zeros((128, 128), F32)
            for j in range(3):
                score = dot(g_t, v_s[j, hs, :])
                tail = jnp.concatenate([score[:, 128:], jnp.zeros((128, 256 - CELLS), F32)], axis=1)
                a = jnp.take_along_axis(score[:, :128], first, axis=1, mode="promise_in_bounds")
                b = jnp.take_along_axis(tail, rest, axis=1, mode="promise_in_bounds")
                val = jnp.where(r < 128, a, b)
                if j == 0:
                    pick = val
                elif j == 1:
                    pick = jnp.where(over1, val, pick)
                else:
                    pick = jnp.where(over2, val, pick)
            rep_s[...] = pick.T[:64] * cw[g]
            ag = jnp.zeros((PTS, 128), F32)
            for c in range(4):
                ag = ag + rep_s[pl.ds(c, PTS, stride=4), :]
            lgs.append(att[g] * (ag - jnp.sum(att[g] * ag, axis=0, keepdims=True)))
        l0 = jnp.concatenate([lgs[0], lgs[2][:, :TAIL]], axis=1)
        l1 = jnp.concatenate([lgs[1], lgs[2][:, TAIL : 2 * TAIL]], axis=1)
        ks = pl.ds(pl.multiple_of(i * 2 * PTS, 2 * PTS), 2 * PTS)
        lg_ref[ks, :] = jnp.concatenate([l0, l1], axis=0).astype(BF)
        return carry

    lax.fori_loop(0, HEADS // 2, pair, 0)
    low_ref[...] = vg_s[0]
    own_ref[...] = vg_s[1]
    high_ref[...] = vg_s[2]
    gv = dot(x_ref[0], vg_s[0], 1, 1)
    gv = gv + dot(x, vg_s[1], 1, 1)
    gv = gv + dot(x_ref[2], vg_s[2], 1, 1)
    gv_ref[...] = gv
    gl_ref[...] = dot(x, lg_ref[...], 1, 1)
    go_ref[...] = dot(samp_s[...], og, 1, 1)


def local_pass(x3, rows, cw, og, vw, lw, ow):
    vm = pl.BlockSpec(memory_space=pltpu.VMEM)
    return pl.pallas_call(
        local_kernel,
        out_shape=(
            jax.ShapeDtypeStruct((D, CELLS), BF),
            jax.ShapeDtypeStruct((D, CELLS), BF),
            jax.ShapeDtypeStruct((D, CELLS), BF),
            jax.ShapeDtypeStruct((HEADS * PTS, CELLS), BF),
            jax.ShapeDtypeStruct((D, D), F32),
            jax.ShapeDtypeStruct((D, HEADS * PTS), F32),
            jax.ShapeDtypeStruct((D, D), F32),
        ),
        in_specs=[vm] * 7,
        out_specs=[vm] * 7,
        scratch_shapes=[
            pltpu.VMEM((3, D, CELLS), BF),
            pltpu.VMEM((HEADS, PTS, CELLS), F32),
            pltpu.VMEM((D, CELLS), F32),
            pltpu.VMEM((D, CELLS), BF),
            pltpu.VMEM((64, 128), F32),
            pltpu.VMEM((3, D, CELLS), BF),
            pltpu.VMEM((4, 64, LANES), F32),
            pltpu.VMEM((3, PAD, LANES), BF),
        ],
        name="local_pass",
    )(x3, rows, cw, og, vw, lw, ow)


def body(features, corner_rows, corner_weights, out_grad, vw, lw, ow):
    x = features[0]
    og = out_grad[0]
    count = lax.axis_size("band")
    up = [(i, (i + 1) % count) for i in range(count)]
    down = [(i, (i - 1) % count) for i in range(count)]
    below = lax.ppermute(x, "band", up)
    above = lax.ppermute(x, "band", down)
    x3 = jnp.stack([below, x, above])
    low, own, high, lg, gv, gl, go = local_pass(
        x3, corner_rows[0], corner_weights[0], og, vw, lw, ow
    )
    from_above = lax.ppermute(low, "band", down)
    from_below = lax.ppermute(high, "band", up)
    value_grad = (
        own.astype(F32) + from_above.astype(F32) + from_below.astype(F32)
    ).astype(BF)
    input_grad = dot(vw, value_grad) + dot(lw, lg)
    flat = jnp.concatenate([gv, gl, go], axis=1)
    total = lax.psum(flat, ("dp", "band"))
    scale = 1.0 / float(lax.axis_size("dp") * count * CELLS) ** 0.5
    total = total * scale
    return (
        input_grad.astype(BF)[None],
        total[:, :D],
        total[:, D : D + HEADS * PTS],
        total[:, D + HEADS * PTS :],
    )


def solution(mesh):
    placed = (
        P("dp", None, "band"),
        P("dp", None, None, "band"),
        P("dp", None, None, "band"),
        P("dp", None, "band"),
        P(),
        P(),
        P(),
    )
    return jax.shard_map(
        body,
        mesh=mesh,
        in_specs=placed,
        out_specs=(P("dp", None, "band"), P(), P(), P()),
        check_vma=False,
    )
```

```python
import jax
import jax.numpy as jnp
from jax import lax
from jax.experimental import pallas as pl
from jax.experimental.pallas import tpu as pltpu
from jax.sharding import PartitionSpec as P

HEADS = 8
LEVELS = 4
POINTS = 4
D = 256
CELLS = 172
PAD = 176
TAIL = CELLS - 128
GAP = 128 - 2 * TAIL
LANES = 384
COLS = 640
HEAD = D // HEADS
PTS = LEVELS * POINTS
BF = jnp.bfloat16
F32 = jnp.float32


def dot(a, b, ca=1, cb=0):
    return lax.dot_general(a, b, (((ca,), (cb,)), ((), ())), preferred_element_type=F32)


def whole_kernel(
    x_ref,
    rows_hbm,
    cw_hbm,
    og_ref,
    vw_ref,
    lw_ref,
    ow_ref,
    ig_ref,
    gv_ref,
    gl_ref,
    go_ref,
    rows_ref,
    cw_ref,
    halo_s,
    v_s,
    att_s,
    g_s,
    samp_s,
    rep_s,
    own_s,
    vg_s,
    wide_s,
    m_s,
    lg_s,
    back_s,
    w_s,
    cs_s,
    cr_s,
    ps_s,
    pr_s,
    yr_s,
    ag_s,
    in_sem,
    halo_sem,
    back_sem,
    core_sem,
    ps_sem,
    pr_sem,
    ys_sem,
    yr_sem,
    as_sem,
    ar_sem,
    rs_sem,
    rr_sem,
):
    band = lax.axis_index("band")
    image = lax.axis_index("dp")
    bands = lax.axis_size("band")
    images = lax.axis_size("dp")
    chips = bands // 2
    core = lax.rem(band, 2)
    chip = lax.div(band, 2)
    up = {"band": lax.rem(band + 1, bands)}
    down = {"band": lax.rem(band + bands - 1, bands)}
    partner = {"band": band + 1 - 2 * core}

    def peer(t):
        return lax.rem(chip + t, chips)

    def remote(src, dst, send, recv, where):
        return pltpu.make_async_remote_copy(
            src_ref=src,
            dst_ref=dst,
            send_sem=send,
            recv_sem=recv,
            device_id=where,
            device_id_type=pl.DeviceIdType.MESH,
        )

    def each(low, high, step):
        def run(t, carry):
            step(t)
            return carry

        lax.fori_loop(low, high, run, 0)

    barrier = pltpu.get_barrier_semaphore()

    def greet(where):
        pl.semaphore_signal(barrier, inc=1, device_id=where, device_id_type=pl.DeviceIdType.MESH)

    greet(up)
    greet(down)
    each(1, chips, lambda t: greet({"band": 2 * peer(t) + core}))
    each(1, images, lambda t: greet({"dp": lax.rem(image + t, images)}))
    rows_in = pltpu.make_async_copy(rows_hbm, rows_ref, in_sem.at[0])
    cw_in = pltpu.make_async_copy(cw_hbm, cw_ref, in_sem.at[1])
    rows_in.start()
    cw_in.start()

    x = x_ref[...]
    og = og_ref[...]
    v_s[1] = dot(vw_ref[...], x, 0, 0).astype(BF)
    logits = dot(lw_ref[...], x, 0, 0)
    att_s[...] = logits.reshape(HEADS, PTS, CELLS)
    g_s[...] = dot(ow_ref[...], og).astype(BF).astype(F32)

    pl.semaphore_wait(barrier, 2 + chips - 1 + images - 1)
    halo_up = remote(x_ref, halo_s.at[0], halo_sem.at[0], halo_sem.at[2], up)
    halo_down = remote(x_ref, halo_s.at[1], halo_sem.at[1], halo_sem.at[3], down)
    halo_up.start()
    halo_down.start()
    rows_in.wait()
    cw_in.wait()
    halo_up.wait()
    halo_down.wait()
    v_s[0] = dot(vw_ref[...], halo_s[0], 0, 0).astype(BF)
    v_s[2] = dot(vw_ref[...], halo_s[1], 0, 0).astype(BF)

    def packed(first, second, rows):
        tail = jnp.concatenate(
            [first[:, 128:], second[:, 128:], jnp.zeros((rows, GAP), first.dtype)], axis=1
        )
        return [first[:, :128], second[:, :128], tail]

    def pair(i, carry):
        h0 = 2 * i
        h1 = 2 * i + 1
        hs = pl.ds(pl.multiple_of(i * 2 * HEAD, 2 * HEAD), 2 * HEAD)
        base = (band - 1) * CELLS
        cells = packed(rows_ref[h0] - base, rows_ref[h1] - base, 64)
        cw = packed(cw_ref[h0], cw_ref[h1], 64)
        logit = packed(att_s[h0], att_s[h1], PTS)
        g0 = g_s[pl.ds(pl.multiple_of(i * 2 * HEAD, HEAD), HEAD), :]
        g1 = g_s[pl.ds(pl.multiple_of(i * 2 * HEAD + HEAD, HEAD), HEAD), :]
        none = jnp.zeros((HEAD, 128), F32)
        gap = jnp.zeros((HEAD, 128 - TAIL), F32)
        top = [g0[:, :128], none, jnp.concatenate([g0[:, 128:], gap], axis=1)]
        bottom = [
            none,
            g1[:, :128],
            jnp.concatenate([none[:, :TAIL], g1[:, 128:], none[:, : 128 - 2 * TAIL]], axis=1),
        ]
        att = []
        for g in range(3):
            e = jnp.exp(logit[g])
            att.append(e / jnp.sum(e, axis=0, keepdims=True))
            for c in range(4):
                rep_s[pl.ds(c, PTS, stride=4), :] = att[g]
            over1 = cells[g] >= CELLS
            over2 = cells[g] >= 2 * CELLS
            r = cells[g] - jnp.where(over2, 2 * CELLS, jnp.where(over1, CELLS, 0))
            w = (rep_s[...] * cw[g]).astype(BF).astype(F32)
            zero = jnp.zeros_like(w)
            ls = slice(g * 128, (g + 1) * 128)
            wide_s[0, :, ls] = r.astype(F32)
            wide_s[1, :, ls] = jnp.where(over1, zero, w)
            wide_s[2, :, ls] = jnp.where(jnp.logical_and(over1, jnp.logical_not(over2)), w, zero)
            wide_s[3, :, ls] = jnp.where(over2, w, zero)

        def wide(n, k):
            row = jnp.broadcast_to(wide_s[n, pl.ds(k, 1), :], (16, LANES))
            return row.astype(BF)

        sub = lax.broadcasted_iota(jnp.int32, (16, LANES), 0)
        for cb in range(11):
            if cb < 8:
                levels = (0,)
            elif cb < 10:
                levels = (1,)
            else:
                levels = (2, 3)
            ids = (sub + cb * 16).astype(F32).astype(BF)
            acc = [jnp.zeros((16, LANES), BF) for _ in range(3)]
            for lev in levels:
                for k in range(lev * 16, lev * 16 + 16):
                    hit = wide(0, k) == ids
                    for j in range(3):
                        acc[j] = acc[j] + jnp.where(hit, wide(1 + j, k), jnp.zeros((), BF))
            for j in range(3):
                m_s[j, cb * 16 : cb * 16 + 16, :] = acc[j]

        gp = jnp.concatenate(
            [jnp.concatenate(top, axis=1), jnp.concatenate(bottom, axis=1)], axis=0
        ).astype(BF)
        samp = jnp.zeros((2 * HEAD, LANES), F32)
        for j in range(3):
            m_j = m_s[j, :CELLS, :]
            samp = samp + dot(v_s[j, hs, :], m_j)
            part = dot(gp, m_j, 1, 1)
            if j == 1:
                own_s[hs, :] = part
            vg_s[j, hs, :] = part.astype(BF)
        s0 = jnp.concatenate([samp[:HEAD, :128], samp[:HEAD, 256 : 256 + TAIL]], axis=1)
        s1 = jnp.concatenate(
            [samp[HEAD:, 128:256], samp[HEAD:, 256 + TAIL : 256 + 2 * TAIL]], axis=1
        )
        samp_s[hs, :] = jnp.concatenate([s0, s1], axis=0).astype(BF)

        lgs = []
        for g in range(3):
            at = jnp.concatenate([cells[g], jnp.zeros((64, 128), jnp.int32)], axis=0).T
            over1 = at >= CELLS
            over2 = at >= 2 * CELLS
            r = at - jnp.where(over2, 2 * CELLS, jnp.where(over1, CELLS, 0))
            first = jnp.clip(r, 0, 127)
            rest = jnp.clip(r - 128, 0, 127)
            g_t = jnp.concatenate([top[g], bottom[g]], axis=0).T.astype(BF)
            pick = jnp.zeros((128, 128), F32)
            for j in range(3):
                score = dot(g_t, v_s[j, hs, :])
                tail = jnp.concatenate([score[:, 128:], jnp.zeros((128, 256 - CELLS), F32)], axis=1)
                a = jnp.take_along_axis(score[:, :128], first, axis=1, mode="promise_in_bounds")
                b = jnp.take_along_axis(tail, rest, axis=1, mode="promise_in_bounds")
                val = jnp.where(r < 128, a, b)
                if j == 0:
                    pick = val
                elif j == 1:
                    pick = jnp.where(over1, val, pick)
                else:
                    pick = jnp.where(over2, val, pick)
            rep_s[...] = pick.T[:64] * cw[g]
            ag = jnp.zeros((PTS, 128), F32)
            for c in range(4):
                ag = ag + rep_s[pl.ds(c, PTS, stride=4), :]
            lgs.append(att[g] * (ag - jnp.sum(att[g] * ag, axis=0, keepdims=True)))
        l0 = jnp.concatenate([lgs[0], lgs[2][:, :TAIL]], axis=1)
        l1 = jnp.concatenate([lgs[1], lgs[2][:, TAIL : 2 * TAIL]], axis=1)
        ks = pl.ds(pl.multiple_of(i * 2 * PTS, 2 * PTS), 2 * PTS)
        lg_s[ks, :] = jnp.concatenate([l0, l1], axis=0).astype(BF)
        return carry

    lax.fori_loop(0, HEADS // 2, pair, 0)
    back_down = remote(vg_s.at[0], back_s.at[1], back_sem.at[0], back_sem.at[2], down)
    back_up = remote(vg_s.at[2], back_s.at[0], back_sem.at[1], back_sem.at[3], up)
    back_down.start()
    back_up.start()

    gv = dot(halo_s[0], vg_s[0], 1, 1)
    gv = gv + dot(x, vg_s[1], 1, 1)
    gv = gv + dot(halo_s[1], vg_s[2], 1, 1)
    w_s[:, :D] = gv
    w_s[:, D : D + 128] = dot(x, lg_s[...], 1, 1)
    w_s[:, D + 128 :] = dot(samp_s[...], og, 1, 1)

    mine = pl.ds(pl.multiple_of(core * 128, 128), 128)
    other = pl.ds(pl.multiple_of(128 - core * 128, 128), 128)
    cs_s[...] = w_s[other, :].astype(BF)
    swap = remote(cs_s, cr_s, core_sem.at[0], core_sem.at[1], partner)
    swap.start()
    swap.wait()
    half = w_s[mine, :] + cr_s[...].astype(F32)
    w_s[mine, :] = half
    ps_s[...] = half.astype(BF).reshape(16, 8, COLS)

    def spread(t):
        q = peer(t)
        return remote(
            ps_s.at[q], pr_s.at[chip], ps_sem.at[t], pr_sem.at[chip], {"band": 2 * q + core}
        )

    def gathered(t):
        q = peer(t)
        return remote(
            ps_s.at[q], pr_s.at[q], ps_sem.at[t], pr_sem.at[q], {"band": 2 * q + core}
        )

    each(1, chips, lambda t: spread(t).start())

    back_down.wait()
    back_up.wait()
    value_grad = own_s[...] + back_s[0].astype(F32) + back_s[1].astype(F32)
    input_grad = dot(vw_ref[...], value_grad.astype(BF)) + dot(lw_ref[...], lg_s[...])
    ig_ref[...] = input_grad.astype(BF)

    def add(t, total):
        gathered(t).wait_recv()
        return total + pr_s[peer(t)].astype(F32)

    at = pl.multiple_of(core * 128 + chip * 8, 8)
    total = lax.fori_loop(1, chips, add, w_s[pl.ds(at, 8), :])
    yr_s[image] = total

    def across(t, slot):
        q = lax.rem(image + t, images)
        return remote(
            yr_s.at[image], yr_s.at[q if slot else image], ys_sem.at[t],
            yr_sem.at[q if slot else image], {"dp": q},
        )

    each(1, images, lambda t: across(t, False).start())
    each(1, images, lambda t: across(t, True).wait_recv())
    total = yr_s[0]
    for n in range(1, images):
        total = total + yr_s[n]
    scale = 1.0 / float(images * bands * CELLS) ** 0.5
    ag_s[core, chip] = (total * scale).astype(BF)

    def share(t):
        q = peer(t)
        spot = ag_s.at[core, chip]
        return remote(spot, spot, as_sem.at[t], ar_sem.at[chip], {"band": 2 * q + core})

    def shared(t):
        q = peer(t)
        spot = ag_s.at[core, q]
        return remote(spot, spot, as_sem.at[t], ar_sem.at[q], {"band": 2 * q + core})

    def relay(t):
        q = peer(t)
        spot = ag_s.at[core, q]
        return remote(spot, spot, rs_sem.at[q], rr_sem.at[q], partner)

    def relayed(t):
        q = peer(t)
        spot = ag_s.at[1 - core, q]
        return remote(spot, spot, rs_sem.at[q], rr_sem.at[q], partner)

    each(1, chips, lambda t: share(t).start())
    relay(0).start()

    def forward(t):
        shared(t).wait_recv()
        relay(t).start()

    each(1, chips, forward)
    each(0, chips, lambda t: relayed(t).wait_recv())
    whole = ag_s[...].reshape(D, COLS).astype(F32)
    gv_ref[...] = whole[:, :D]
    gl_ref[...] = whole[:, D : D + 128]
    go_ref[...] = whole[:, D + 128 :]

    each(1, chips, lambda t: spread(t).wait_send())
    each(1, images, lambda t: across(t, False).wait_send())
    each(1, chips, lambda t: share(t).wait_send())
    each(0, chips, lambda t: relay(t).wait_send())


def body(features, corner_rows, corner_weights, out_grad, vw, lw, ow):
    vm = pl.BlockSpec(memory_space=pltpu.VMEM)
    hbm = pl.BlockSpec(memory_space=pl.ANY)
    dma = pltpu.SemaphoreType.DMA
    ig, gv, gl, go = pl.pallas_call(
        whole_kernel,
        out_shape=(
            jax.ShapeDtypeStruct((D, CELLS), BF),
            jax.ShapeDtypeStruct((D, D), F32),
            jax.ShapeDtypeStruct((D, HEADS * PTS), F32),
            jax.ShapeDtypeStruct((D, D), F32),
        ),
        in_specs=[vm, hbm, hbm, vm, vm, vm, vm],
        out_specs=[vm] * 4,
        scratch_shapes=[
            pltpu.VMEM((HEADS, 64, CELLS), jnp.int32),
            pltpu.VMEM((HEADS, 64, CELLS), F32),
            pltpu.VMEM((2, D, CELLS), BF),
            pltpu.VMEM((3, D, CELLS), BF),
            pltpu.VMEM((HEADS, PTS, CELLS), F32),
            pltpu.VMEM((D, CELLS), F32),
            pltpu.VMEM((D, CELLS), BF),
            pltpu.VMEM((64, 128), F32),
            pltpu.VMEM((D, CELLS), F32),
            pltpu.VMEM((3, D, CELLS), BF),
            pltpu.VMEM((4, 64, LANES), F32),
            pltpu.VMEM((3, PAD, LANES), BF),
            pltpu.VMEM((HEADS * PTS, CELLS), BF),
            pltpu.VMEM((2, D, CELLS), BF),
            pltpu.VMEM((D, COLS), F32),
            pltpu.VMEM((128, COLS), BF),
            pltpu.VMEM((128, COLS), BF),
            pltpu.VMEM((16, 8, COLS), BF),
            pltpu.VMEM((16, 8, COLS), BF),
            pltpu.VMEM((4, 8, COLS), F32),
            pltpu.VMEM((2, 16, 8, COLS), BF),
            dma((2,)),
            dma((4,)),
            dma((4,)),
            dma((2,)),
            dma((16,)),
            dma((16,)),
            dma((4,)),
            dma((4,)),
            dma((16,)),
            dma((16,)),
            dma((16,)),
            dma((16,)),
        ],
        compiler_params=pltpu.CompilerParams(collective_id=0, has_side_effects=True),
        name="whole",
    )(features[0], corner_rows[0], corner_weights[0], out_grad[0], vw, lw, ow)
    return (ig[None], gv, gl, go)


def solution(mesh):
    placed = (
        P("dp", None, "band"),
        P("dp", None, None, "band"),
        P("dp", None, None, "band"),
        P("dp", None, "band"),
        P(),
        P(),
        P(),
    )
    return jax.shard_map(
        body,
        mesh=mesh,
        in_specs=placed,
        out_specs=(P("dp", None, "band"), P(), P(), P()),
        check_vma=False,
    )
```

```python
import jax
import jax.numpy as jnp
from jax import lax
from jax.experimental import pallas as pl
from jax.experimental.pallas import tpu as pltpu
from jax.sharding import PartitionSpec as P

HEADS = 8
LEVELS = 4
POINTS = 4
D = 256
CELLS = 172
PAD = 176
TAIL = CELLS - 128
GAP = 128 - 2 * TAIL
LANES = 384
PAIRS = HEADS // 2
HEAD = D // HEADS
PTS = LEVELS * POINTS
ROWS = 2 * D + HEADS * PTS
PIECE = 40
BF = jnp.bfloat16
F32 = jnp.float32
I32 = jnp.int32


def dot(a, b, ca=1, cb=0):
    return lax.dot_general(a, b, (((ca,), (cb,)), ((), ())), preferred_element_type=F32)


def lane_pick(table, index):
    numbers = lax.GatherDimensionNumbers(
        offset_dims=(),
        collapsed_slice_dims=(1,),
        start_index_map=(1,),
        operand_batching_dims=(0,),
        start_indices_batching_dims=(0,),
    )
    return lax.gather(
        table,
        index[..., None],
        numbers,
        slice_sizes=(1, 1),
        mode=lax.GatherScatterMode.PROMISE_IN_BOUNDS,
    )


def whole_kernel(
    x_hbm,
    rows_hbm,
    cw_hbm,
    og_hbm,
    vw_hbm,
    lw_hbm,
    ow_hbm,
    ig_ref,
    ag_ref,
    x_s,
    og_s,
    vw_s,
    lw_s,
    ow_s,
    rows_s,
    cw_s,
    vwt_s,
    halo_s,
    v_s,
    att_s,
    g_s,
    samp_s,
    rep_s,
    own_s,
    vg_s,
    wide_s,
    m_s,
    lg_s,
    send_s,
    back_s,
    w_s,
    cs_s,
    cr_s,
    ps_s,
    pr_s,
    yr_s,
    in_sem,
    halo_sem,
    back_sem,
    core_sem,
    ps_sem,
    pr_sem,
    ys_sem,
    yr_sem,
    as_sem,
    ar_sem,
    rs_sem,
    rr_sem,
):
    band = lax.axis_index("band")
    image = lax.axis_index("dp")
    bands = lax.axis_size("band")
    images = lax.axis_size("dp")
    chips = bands // 2
    core = lax.rem(band, 2)
    chip = lax.div(band, 2)
    up = {"band": lax.rem(band + 1, bands)}
    down = {"band": lax.rem(band + bands - 1, bands)}
    partner = {"band": band + 1 - 2 * core}

    def peer(t):
        return lax.rem(chip + t, chips)

    def remote(src, dst, send, recv, where):
        return pltpu.make_async_remote_copy(
            src_ref=src,
            dst_ref=dst,
            send_sem=send,
            recv_sem=recv,
            device_id=where,
            device_id_type=pl.DeviceIdType.MESH,
        )

    def each(low, high, step):
        def run(t, carry):
            step(t)
            return carry

        lax.fori_loop(low, high, run, 0)

    barrier = pltpu.get_barrier_semaphore()

    def greet(where):
        pl.semaphore_signal(barrier, inc=1, device_id=where, device_id_type=pl.DeviceIdType.MESH)

    loads = [
        pltpu.make_async_copy(src, dst, in_sem.at[n])
        for n, (src, dst) in enumerate(
            [
                (x_hbm, x_s),
                (lw_hbm, lw_s),
                (rows_hbm, rows_s),
                (cw_hbm, cw_s),
                (vw_hbm, vw_s),
                (og_hbm, og_s),
                (ow_hbm, ow_s),
            ]
        )
    ]
    for load in loads:
        load.start()
    greet(up)
    greet(down)
    each(1, chips, lambda t: greet({"band": 2 * peer(t) + core}))
    each(1, images, lambda t: greet({"dp": lax.rem(image + t, images)}))

    loads[0].wait()
    loads[1].wait()
    x = x_s[...]
    att_s[...] = dot(lw_s[...].T, x, 1, 1).reshape(HEADS, PTS, CELLS)
    loads[2].wait()
    loads[3].wait()

    def packed(first, second):
        tail = jnp.concatenate(
            [first[:, 128:], second[:, 128:], jnp.zeros((first.shape[0], GAP), first.dtype)],
            axis=1,
        )
        return [first[:, :128], second[:, :128], tail]

    sub = lax.broadcasted_iota(I32, (16, 128), 0)
    ids = [(sub + cb * 16).astype(F32).astype(BF) for cb in range(11)]
    base = (band - 1) * CELLS
    nil = jnp.zeros((), BF)

    def build(i):
        cells = packed(rows_s[2 * i] - base, rows_s[2 * i + 1] - base)
        cw = packed(cw_s[2 * i], cw_s[2 * i + 1])
        logit = packed(att_s[2 * i], att_s[2 * i + 1])
        att = []
        for g in range(3):
            e = jnp.exp(logit[g])
            att.append(e / jnp.sum(e, axis=0, keepdims=True))
            rep = rep_s.at[(i % 2) * 6 + g]
            for c in range(4):
                rep[pl.ds(c, PTS, stride=4), :] = att[g]
            over1 = cells[g] >= CELLS
            over2 = cells[g] >= 2 * CELLS
            r = cells[g] - jnp.where(over2, 2 * CELLS, jnp.where(over1, CELLS, 0))
            w = (rep[...] * cw[g]).astype(BF).astype(F32)
            zero = jnp.zeros_like(w)
            wide = wide_s.at[i % 2, g]
            wide[0] = r.astype(F32)
            wide[1] = jnp.where(over1, zero, w)
            wide[2] = jnp.where(over1, jnp.where(over2, zero, w), zero)
            wide[3] = jnp.where(over2, w, zero)
            for cbs, levels in ((range(8), (0,)), (range(8, 10), (1,)), (range(10, 11), (2, 3))):
                acc = [[None] * 3 for _ in cbs]
                for lev in levels:
                    for k in range(lev * 16, lev * 16 + 16):
                        row = [
                            jnp.broadcast_to(wide[n, pl.ds(k, 1), :], (16, 128)).astype(BF)
                            for n in range(4)
                        ]
                        for at, cb in enumerate(cbs):
                            hit = row[0] == ids[cb]
                            for j in range(3):
                                term = jnp.where(hit, row[1 + j], nil)
                                old = acc[at][j]
                                acc[at][j] = term if old is None else old + term
                for at, cb in enumerate(cbs):
                    for j in range(3):
                        m_s[i, j, cb * 16 : cb * 16 + 16, g * 128 : (g + 1) * 128] = acc[at][j]
        return cells, cw, att

    def project(i, built):
        cells, cw, att = built
        hs = slice(i * 2 * HEAD, (i + 1) * 2 * HEAD)
        g0 = g_s[i * 2 * HEAD : i * 2 * HEAD + HEAD, :]
        g1 = g_s[i * 2 * HEAD + HEAD : (i + 1) * 2 * HEAD, :]
        none = jnp.zeros((HEAD, 128), F32)
        top = [
            g0[:, :128],
            none,
            jnp.concatenate([g0[:, 128:], none[:, : 128 - TAIL]], axis=1),
        ]
        bottom = [
            none,
            g1[:, :128],
            jnp.concatenate([none[:, :TAIL], g1[:, 128:], none[:, : 128 - 2 * TAIL]], axis=1),
        ]
        gp = jnp.concatenate(
            [jnp.concatenate(top, axis=1), jnp.concatenate(bottom, axis=1)], axis=0
        ).astype(BF)
        samp = jnp.zeros((2 * HEAD, LANES), F32)
        for j in range(3):
            m_j = m_s[i, j, :CELLS, :]
            samp = samp + dot(v_s[j, hs, :], m_j)
            part = dot(gp, m_j, 1, 1)
            if j == 1:
                own_s[hs, :] = part
            vg_s[j, hs, :] = part.astype(BF)
        s0 = jnp.concatenate([samp[:HEAD, :128], samp[:HEAD, 256 : 256 + TAIL]], axis=1)
        s1 = jnp.concatenate(
            [samp[HEAD:, 128:256], samp[HEAD:, 256 + TAIL : 256 + 2 * TAIL]], axis=1
        )
        samp_s[hs, :] = jnp.concatenate([s0, s1], axis=0).astype(BF)

        lgs = []
        for g in range(3):
            at = jnp.concatenate([cells[g], jnp.zeros((64, 128), I32)], axis=0).T
            over1 = at >= CELLS
            over2 = at >= 2 * CELLS
            r = at - jnp.where(over2, 2 * CELLS, jnp.where(over1, CELLS, 0))
            index = jnp.bitwise_and(r, 127)
            near = r < 128
            g_t = jnp.concatenate([top[g], bottom[g]], axis=0).T.astype(BF)
            pick = None
            for j in range(3):
                score = dot(g_t, v_s[j, hs, :])
                tail = jnp.concatenate([score[:, 128:], jnp.zeros((128, 256 - CELLS), F32)], axis=1)
                val = jnp.where(near, lane_pick(score[:, :128], index), lane_pick(tail, index))
                if j == 0:
                    pick = val
                elif j == 1:
                    pick = jnp.where(over1, val, pick)
                else:
                    pick = jnp.where(over2, val, pick)
            rep = rep_s.at[(i % 2) * 6 + 3 + g]
            rep[...] = pick.T[:64] * cw[g]
            ag = jnp.zeros((PTS, 128), F32)
            for c in range(4):
                ag = ag + rep[pl.ds(c, PTS, stride=4), :]
            lgs.append(att[g] * (ag - jnp.sum(att[g] * ag, axis=0, keepdims=True)))
        l0 = jnp.concatenate([lgs[0], lgs[2][:, :TAIL]], axis=1)
        l1 = jnp.concatenate([lgs[1], lgs[2][:, TAIL : 2 * TAIL]], axis=1)
        lg_s[i * 2 * PTS : (i + 1) * 2 * PTS, :] = jnp.concatenate([l0, l1], axis=0).astype(BF)

    built = [build(0)]

    pl.semaphore_wait(barrier, 2 + chips - 1 + images - 1)
    halo_up = remote(x_s, halo_s.at[0], halo_sem.at[0], halo_sem.at[2], up)
    halo_down = remote(x_s, halo_s.at[1], halo_sem.at[1], halo_sem.at[3], down)
    halo_up.start()
    halo_down.start()

    for load in loads[4:]:
        load.wait()
    built.append(build(1))
    vwt_s[...] = vw_s[...].T
    og = og_s[...]
    g_s[...] = dot(ow_s[...], og, 1, 1).astype(BF).astype(F32)
    v_s[1] = dot(vwt_s[...], x, 1, 1).astype(BF)

    halo_up.wait()
    halo_down.wait()

    v_s[0] = dot(vwt_s[...], halo_s[0], 1, 1).astype(BF)
    v_s[2] = dot(vwt_s[...], halo_s[1], 1, 1).astype(BF)
    for i in range(PAIRS):
        project(i, built[i])
        if i + 2 < PAIRS:
            built.append(build(i + 2))

    send_s[0] = vg_s[0].T
    send_s[1] = vg_s[2].T
    back_down = remote(send_s.at[0], back_s.at[1], back_sem.at[0], back_sem.at[2], down)
    back_up = remote(send_s.at[1], back_s.at[0], back_sem.at[1], back_sem.at[3], up)
    back_down.start()
    back_up.start()

    gv = dot(vg_s[0], halo_s[0])
    gv = gv + dot(vg_s[1], x)
    gv = gv + dot(vg_s[2], halo_s[1])
    gl = dot(lg_s[...], x)
    go = dot(samp_s[...], og)
    for c in range(2):
        cols = slice(c * 128, (c + 1) * 128)
        w_s[c, :D, :] = gv[:, cols]
        w_s[c, D : D + HEADS * PTS, :] = gl[:, cols]
        w_s[c, D + HEADS * PTS :, :] = go[:, cols]

    cs_s[...] = w_s[1 - core].astype(BF)
    swap = remote(cs_s, cr_s, core_sem.at[0], core_sem.at[1], partner)
    swap.start()
    swap.wait()
    half = w_s[core] + cr_s[...].astype(F32)
    w_s[core] = half
    ps_s[...] = half.astype(BF).reshape(16, PIECE, 128)

    def spread(t):
        q = peer(t)
        return remote(
            ps_s.at[q], pr_s.at[chip], ps_sem.at[t], pr_sem.at[chip], {"band": 2 * q + core}
        )

    def gathered(t):
        q = peer(t)
        return remote(ps_s.at[q], pr_s.at[q], ps_sem.at[t], pr_sem.at[q], {"band": 2 * q + core})

    each(1, chips, lambda t: spread(t).start())

    back_down.wait()
    back_up.wait()
    value_grad = own_s[...].T + back_s[0].astype(F32) + back_s[1].astype(F32)
    input_grad = dot(value_grad.astype(BF), vwt_s[...]) + dot(
        lg_s[...].astype(F32).T.astype(BF), lw_s[...], 1, 1
    )
    ig_ref[...] = input_grad.astype(BF)

    def add(t, total):
        gathered(t).wait_recv()
        return total + pr_s[peer(t)].astype(F32)

    at = pl.multiple_of(chip * PIECE, 8)
    total = lax.fori_loop(1, chips, add, w_s[core, pl.ds(at, PIECE), :])

    yr_s[image] = total

    def across(t, slot):
        q = lax.rem(image + t, images)
        n = q if slot else image
        return remote(yr_s.at[image], yr_s.at[n], ys_sem.at[t], yr_sem.at[n], {"dp": q})

    each(1, images, lambda t: across(t, False).start())
    each(1, images, lambda t: across(t, True).wait_recv())
    total = yr_s[0]
    for n in range(1, images):
        total = total + yr_s[n]
    scale = 1.0 / float(images * bands * CELLS) ** 0.5
    ag_ref[core, chip] = (total * scale).astype(BF)

    def share(t, slot):
        q = peer(t)
        spot = ag_ref.at[core, q if slot else chip]
        return remote(
            spot, spot, as_sem.at[t], ar_sem.at[q if slot else chip], {"band": 2 * q + core}
        )

    def relay(t, side):
        q = peer(t)
        spot = ag_ref.at[side, q]
        return remote(spot, spot, rs_sem.at[q], rr_sem.at[q], partner)

    each(1, chips, lambda t: share(t, False).start())
    relay(0, core).start()

    def forward(t):
        share(t, True).wait_recv()
        relay(t, core).start()

    each(1, chips, forward)
    each(0, chips, lambda t: relay(t, 1 - core).wait_recv())

    each(1, chips, lambda t: spread(t).wait_send())
    each(1, images, lambda t: across(t, False).wait_send())
    each(1, chips, lambda t: share(t, False).wait_send())
    each(0, chips, lambda t: relay(t, core).wait_send())


def finish_kernel(ag_ref, ig_in, ig_ref, gv_ref, gl_ref, go_ref):
    ig_ref[...] = ig_in[...]
    for c in range(2):
        cols = slice(c * 128, (c + 1) * 128)
        part = ag_ref[c].reshape(ROWS, 128).astype(F32)
        gv_ref[cols, :] = part[:D].T
        gl_ref[cols, :] = part[D : D + HEADS * PTS].T
        go_ref[:, cols] = part[D + HEADS * PTS :]


def body(features, corner_rows, corner_weights, out_grad, vw, lw, ow):
    vm = pl.BlockSpec(memory_space=pltpu.VMEM)
    hbm = pl.BlockSpec(memory_space=pltpu.HBM)
    dma = pltpu.SemaphoreType.DMA
    ig, ag = pl.pallas_call(
        whole_kernel,
        out_shape=(
            pltpu.VMEM((CELLS, D), BF),
            pltpu.VMEM((2, 16, PIECE, 128), BF),
        ),
        in_specs=[hbm] * 7,
        out_specs=[vm] * 2,
        scratch_shapes=[
            pltpu.VMEM((CELLS, D), BF),
            pltpu.VMEM((CELLS, D), BF),
            pltpu.VMEM((D, D), BF),
            pltpu.VMEM((D, HEADS * PTS), BF),
            pltpu.VMEM((D, D), BF),
            pltpu.VMEM((HEADS, 64, CELLS), I32),
            pltpu.VMEM((HEADS, 64, CELLS), F32),
            pltpu.VMEM((D, D), BF),
            pltpu.VMEM((2, CELLS, D), BF),
            pltpu.VMEM((3, D, CELLS), BF),
            pltpu.VMEM((HEADS, PTS, CELLS), F32),
            pltpu.VMEM((D, CELLS), F32),
            pltpu.VMEM((D, CELLS), BF),
            pltpu.VMEM((12, 64, 128), F32),
            pltpu.VMEM((D, CELLS), F32),
            pltpu.VMEM((3, D, CELLS), BF),
            pltpu.VMEM((2, 3, 4, 64, 128), F32),
            pltpu.VMEM((PAIRS, 3, PAD, LANES), BF),
            pltpu.VMEM((HEADS * PTS, CELLS), BF),
            pltpu.VMEM((2, CELLS, D), BF),
            pltpu.VMEM((2, CELLS, D), BF),
            pltpu.VMEM((2, ROWS, 128), F32),
            pltpu.VMEM((ROWS, 128), BF),
            pltpu.VMEM((ROWS, 128), BF),
            pltpu.VMEM((16, PIECE, 128), BF),
            pltpu.VMEM((16, PIECE, 128), BF),
            pltpu.VMEM((4, PIECE, 128), F32),
            dma((7,)),
            dma((4,)),
            dma((4,)),
            dma((2,)),
            dma((16,)),
            dma((16,)),
            dma((4,)),
            dma((4,)),
            dma((16,)),
            dma((16,)),
            dma((16,)),
            dma((16,)),
        ],
        compiler_params=pltpu.CompilerParams(
            collective_id=0, has_side_effects=True, vmem_limit_bytes=60 * 10**6
        ),
        name="whole",
    )(
        features[0].T,
        corner_rows[0],
        corner_weights[0],
        out_grad[0].T,
        vw,
        lw,
        ow,
    )
    ig, gv, gl, go = pl.pallas_call(
        finish_kernel,
        out_shape=(
            jax.ShapeDtypeStruct((CELLS, D), BF),
            jax.ShapeDtypeStruct((D, D), F32),
            jax.ShapeDtypeStruct((D, HEADS * PTS), F32),
            jax.ShapeDtypeStruct((D, D), F32),
        ),
        in_specs=[vm] * 2,
        out_specs=[vm] * 4,
        compiler_params=pltpu.CompilerParams(vmem_limit_bytes=8 * 2**20),
        name="finish",
    )(ag, ig)
    return (ig.T[None], gv, gl, go)


def solution(mesh):
    placed = (
        P("dp", None, "band"),
        P("dp", None, None, "band"),
        P("dp", None, None, "band"),
        P("dp", None, "band"),
        P(),
        P(),
        P(),
    )
    return jax.shard_map(
        body,
        mesh=mesh,
        in_specs=placed,
        out_specs=(P("dp", None, "band"), P(), P(), P()),
        check_vma=False,
    )
```

```python
import jax
import jax.numpy as jnp
from jax import lax
from jax.experimental import pallas as pl
from jax.experimental.pallas import tpu as pltpu
from jax.sharding import PartitionSpec as P

HEADS = 8
LEVELS = 4
POINTS = 4
D = 256
CELLS = 172
PAD = 176
TAIL = CELLS - 128
GAP = 128 - 2 * TAIL
LANES = 384
PAIRS = HEADS // 2
HEAD = D // HEADS
PTS = LEVELS * POINTS
CHUNKS = (256, 256, 128)
BF = jnp.bfloat16
F32 = jnp.float32
I32 = jnp.int32


def dot(a, b, ca=1, cb=0):
    return lax.dot_general(a, b, (((ca,), (cb,)), ((), ())), preferred_element_type=F32)


def lane_pick(table, index):
    numbers = lax.GatherDimensionNumbers(
        offset_dims=(),
        collapsed_slice_dims=(1,),
        start_index_map=(1,),
        operand_batching_dims=(0,),
        start_indices_batching_dims=(0,),
    )
    return lax.gather(
        table,
        index[..., None],
        numbers,
        slice_sizes=(1, 1),
        mode=lax.GatherScatterMode.PROMISE_IN_BOUNDS,
    )


def whole_kernel(
    x_hbm,
    rows_hbm,
    cw_hbm,
    og_hbm,
    vw_hbm,
    lw_hbm,
    ow_hbm,
    ig_ref,
    aga_ref,
    agb_ref,
    agc_ref,
    x_s,
    og_s,
    vw_s,
    lw_s,
    ow_s,
    rows_s,
    cw_s,
    vwt_s,
    halo_s,
    v_s,
    att_s,
    g_s,
    samp_s,
    rep_s,
    own_s,
    vg_s,
    wide_s,
    m_s,
    lg_s,
    send_s,
    back_s,
    gp_s,
    gt_s,
    half_s,
    at_s,
    pick_s,
    w_s,
    cs_s,
    cr_s,
    ps_s,
    pr_s,
    yr_s,
    in_sem,
    halo_sem,
    back_sem,
    core_sem,
    ps_sem,
    pr_sem,
    ys_sem,
    yr_sem,
    as_sem,
    ar_sem,
    rs_sem,
    rr_sem,
):
    ag_refs = (aga_ref, agb_ref, agc_ref)
    band = lax.axis_index("band")
    image = lax.axis_index("dp")
    bands = lax.axis_size("band")
    images = lax.axis_size("dp")
    chips = bands // 2
    core = lax.rem(band, 2)
    chip = lax.div(band, 2)
    up = {"band": lax.rem(band + 1, bands)}
    down = {"band": lax.rem(band + bands - 1, bands)}
    partner = {"band": band + 1 - 2 * core}

    def peer(t):
        return lax.rem(chip + t, chips)

    def remote(src, dst, send, recv, where):
        return pltpu.make_async_remote_copy(
            src_ref=src,
            dst_ref=dst,
            send_sem=send,
            recv_sem=recv,
            device_id=where,
            device_id_type=pl.DeviceIdType.MESH,
        )

    def each(low, high, step):
        def run(t, carry):
            step(t)
            return carry

        lax.fori_loop(low, high, run, 0)

    barrier = pltpu.get_barrier_semaphore()

    def greet(where):
        pl.semaphore_signal(barrier, inc=1, device_id=where, device_id_type=pl.DeviceIdType.MESH)

    first, rest = pl.ds(0, 2), pl.ds(2, HEADS - 2)
    loads = [
        pltpu.make_async_copy(src, dst, in_sem.at[n])
        for n, (src, dst) in enumerate(
            [
                (x_hbm, x_s),
                (lw_hbm, lw_s),
                (rows_hbm.at[first], rows_s.at[first]),
                (cw_hbm.at[first], cw_s.at[first]),
                (vw_hbm, vw_s),
                (og_hbm, og_s),
                (ow_hbm, ow_s),
                (rows_hbm.at[rest], rows_s.at[rest]),
                (cw_hbm.at[rest], cw_s.at[rest]),
            ]
        )
    ]
    for load in loads:
        load.start()
    each(1, bands, lambda t: greet({"band": lax.rem(band + t, bands)}))
    each(1, images, lambda t: greet({"dp": lax.rem(image + t, images)}))

    loads[0].wait()
    loads[1].wait()
    x = x_s[...]
    att_s[...] = dot(lw_s[...].T, x, 1, 1).reshape(HEADS, PTS, CELLS)
    loads[2].wait()
    loads[3].wait()

    def packed(first, second):
        tail = jnp.concatenate(
            [first[:, 128:], second[:, 128:], jnp.zeros((first.shape[0], GAP), first.dtype)],
            axis=1,
        )
        return [first[:, :128], second[:, :128], tail]

    sub = lax.broadcasted_iota(I32, (16, 128), 0)
    ids = [(sub + cb * 16).astype(F32).astype(BF) for cb in range(11)]
    base = (band - 1) * CELLS
    nil = jnp.zeros((), BF)

    def build(i):
        cells = packed(rows_s[2 * i] - base, rows_s[2 * i + 1] - base)
        cw = packed(cw_s[2 * i], cw_s[2 * i + 1])
        logit = packed(att_s[2 * i], att_s[2 * i + 1])
        att = []
        for g in range(3):
            e = jnp.exp(logit[g])
            att.append(e / jnp.sum(e, axis=0, keepdims=True))
            rep = rep_s.at[(i % 2) * 6 + g]
            for c in range(4):
                rep[pl.ds(c, PTS, stride=4), :] = att[g]
            over1 = cells[g] >= CELLS
            over2 = cells[g] >= 2 * CELLS
            r = cells[g] - jnp.where(over2, 2 * CELLS, jnp.where(over1, CELLS, 0))
            w = (rep[...] * cw[g]).astype(BF).astype(F32)
            zero = jnp.zeros_like(w)
            wide = wide_s.at[i % 2, g]
            wide[0] = r.astype(F32)
            wide[1] = jnp.where(over1, zero, w)
            wide[2] = jnp.where(over1, jnp.where(over2, zero, w), zero)
            wide[3] = jnp.where(over2, w, zero)
            for cbs, levels in ((range(8), (0,)), (range(8, 10), (1,)), (range(10, 11), (2, 3))):
                acc = [[None] * 3 for _ in cbs]
                for lev in levels:
                    for k in range(lev * 16, lev * 16 + 16):
                        row = [
                            jnp.broadcast_to(wide[n, pl.ds(k, 1), :], (16, 128)).astype(BF)
                            for n in range(4)
                        ]
                        for at, cb in enumerate(cbs):
                            hit = row[0] == ids[cb]
                            for j in range(3):
                                term = jnp.where(hit, row[1 + j], nil)
                                old = acc[at][j]
                                acc[at][j] = term if old is None else old + term
                for at, cb in enumerate(cbs):
                    for j in range(3):
                        m_s[i, j, cb * 16 : cb * 16 + 16, g * 128 : (g + 1) * 128] = acc[at][j]
        return cells, cw, att

    def heads_of(i):
        return slice(i * 2 * HEAD, (i + 1) * 2 * HEAD)

    def parts(at):
        over1 = at >= CELLS
        over2 = at >= 2 * CELLS
        r = at - jnp.where(over2, 2 * CELLS, jnp.where(over1, CELLS, 0))
        return over1, over2, r < 128, jnp.bitwise_and(r, 127)

    def spread_grad(i):
        g0 = g_s[i * 2 * HEAD : i * 2 * HEAD + HEAD, :]
        g1 = g_s[i * 2 * HEAD + HEAD : (i + 1) * 2 * HEAD, :]
        none = jnp.zeros((HEAD, 128), F32)
        top = [
            g0[:, :128],
            none,
            jnp.concatenate([g0[:, 128:], none[:, : 128 - TAIL]], axis=1),
        ]
        bottom = [
            none,
            g1[:, :128],
            jnp.concatenate([none[:, :TAIL], g1[:, 128:], none[:, : 128 - 2 * TAIL]], axis=1),
        ]
        for g in range(3):
            both = jnp.concatenate([top[g], bottom[g]], axis=0)
            gp_s[i, :, g * 128 : (g + 1) * 128] = both.astype(BF)
            gt_s[i, g] = both.T.astype(BF)

    def project_own(i):
        hs = heads_of(i)
        m_j = m_s[i, 1, :CELLS, :]
        half_s[i] = dot(v_s[1, hs, :CELLS], m_j)
        part = dot(gp_s[i], m_j, 1, 1)
        own_s[hs, :] = part
        vg_s[1, hs, :] = part.astype(BF)

    def project_beside(i):
        hs = heads_of(i)
        samp = half_s[i]
        for j in (0, 2):
            m_j = m_s[i, j, :CELLS, :]
            samp = samp + dot(v_s[j, hs, :CELLS], m_j)
            vg_s[j, hs, :] = dot(gp_s[i], m_j, 1, 1).astype(BF)
        s0 = jnp.concatenate([samp[:HEAD, :128], samp[:HEAD, 256 : 256 + TAIL]], axis=1)
        s1 = jnp.concatenate(
            [samp[HEAD:, 128:256], samp[HEAD:, 256 + TAIL : 256 + 2 * TAIL]], axis=1
        )
        samp_s[hs, :] = jnp.concatenate([s0, s1], axis=0).astype(BF)

    def lookup(table, near, index):
        near_part = lane_pick(table[:, :128], index)
        return jnp.where(near, near_part, lane_pick(table[:, 128:], index))

    def groups(g):
        return range(0, 128 if g < 2 else 2 * TAIL, 8)

    def attend_own(i, built):
        for g in range(3):
            at = jnp.concatenate([built[0][g], jnp.zeros((64, 128), I32)], axis=0).T
            at_s[i, g] = at
            score = dot(gt_s[i, g], v_s[1, heads_of(i), :])
            for q in groups(g):
                _, _, near, index = parts(at[q : q + 8])
                pick_s[i, g, q : q + 8, :] = lookup(score[q : q + 8], near, index)

    def attend_beside(i, built):
        _, cw, att = built
        lgs = []
        for g in range(3):
            below = dot(gt_s[i, g], v_s[0, heads_of(i), :])
            above = dot(gt_s[i, g], v_s[2, heads_of(i), :])
            for q in groups(g):
                qs = slice(q, q + 8)
                over1, over2, near, index = parts(at_s[i, g, qs, :])
                pick = jnp.where(over1, pick_s[i, g, qs, :], lookup(below[qs], near, index))
                pick_s[i, g, qs, :] = jnp.where(over2, lookup(above[qs], near, index), pick)
            rep = rep_s.at[(i % 2) * 6 + 3 + g]
            rep[...] = pick_s[i, g, :, :64].T * cw[g]
            ag = jnp.zeros((PTS, 128), F32)
            for c in range(4):
                ag = ag + rep[pl.ds(c, PTS, stride=4), :]
            lgs.append(att[g] * (ag - jnp.sum(att[g] * ag, axis=0, keepdims=True)))
        l0 = jnp.concatenate([lgs[0], lgs[2][:, :TAIL]], axis=1)
        l1 = jnp.concatenate([lgs[1], lgs[2][:, TAIL : 2 * TAIL]], axis=1)
        lg_s[i * 2 * PTS : (i + 1) * 2 * PTS, :] = jnp.concatenate([l0, l1], axis=0).astype(BF)

    scale = 1.0 / float(images * bands * CELLS) ** 0.5

    def weights(n, blocks):
        for c in range(2):
            at = 0
            for block in blocks:
                w_s[n][c, at : at + block.shape[0], :] = block[:, c * 128 : (c + 1) * 128]
                at += block.shape[0]

    def pair_weights(n, pairs):
        first, last = pairs[0] * 2 * HEAD, (pairs[-1] + 1) * 2 * HEAD
        gv = dot(vg_s[0, first:last, :], halo_s[0])
        gv = gv + dot(vg_s[1, first:last, :], x)
        gv = gv + dot(vg_s[2, first:last, :], halo_s[1])
        weights(n, [gv, dot(samp_s[first:last, :], og)])

    def swap(n):
        return remote(cs_s[n], cr_s[n], core_sem.at[n, 0], core_sem.at[n, 1], partner)

    def swap_send(n):
        cs_s[n][...] = w_s[n][1 - core].astype(BF)
        swap(n).start()

    def piece(n, t, where):
        q = peer(t)
        return remote(
            ps_s[n].at[q], pr_s[n].at[chip], ps_sem.at[n], pr_sem.at[n], {"band": 2 * q + core}
        )

    def plane_send(n):
        swap(n).wait()
        half = w_s[n][core] + cr_s[n][...].astype(F32)
        ps_s[n][...] = half.astype(BF).reshape(ps_s[n].shape)
        each(1, chips, lambda t: piece(n, t, None).start())
        pr_s[n][chip] = ps_s[n][chip]

    def bulk(n):
        some = pl.ds(0, 15)
        return remote(
            ps_s[n].at[some], pr_s[n].at[some], ps_sem.at[n], pr_sem.at[n], partner
        )

    def across(n, t):
        q = lax.rem(image + t, images)
        spot = yr_s[n].at[image]
        return remote(spot, spot, ys_sem.at[n], yr_sem.at[n], {"dp": q})

    def across_bulk(n):
        some = yr_s[n].at[pl.ds(0, 3)]
        return remote(some, some, ys_sem.at[n], yr_sem.at[n], partner)

    slot = core * 16 + chip

    def direct(n, t):
        q = lax.rem(band + t, bands)
        return remote(
            ps_s[n].at[lax.rem(q, 2) * 16 + lax.div(q, 2)],
            pr_s[n].at[slot],
            ps_sem.at[n],
            pr_sem.at[n],
            {"band": q},
        )

    def direct_bulk(n):
        some = pl.ds(0, 31)
        return remote(
            ps_s[n].at[some], pr_s[n].at[some], ps_sem.at[n], pr_sem.at[n], partner
        )

    def direct_send(n):
        ps_s[n][...] = w_s[n][...].astype(BF).reshape(ps_s[n].shape)
        each(1, bands, lambda t: direct(n, t).start())
        pr_s[n][slot] = ps_s[n][slot]

    def across_send(n):
        pieces = []
        if n < 2:
            bulk(n).wait_recv()
            pieces = [pr_s[n][q] for q in range(16)]
        else:
            direct_bulk(n).wait_recv()
            pieces = [pr_s[n][q] for q in range(32)]
        sums = [piece.astype(F32) for piece in pieces]
        while len(sums) > 1:
            sums = [a + b for a, b in zip(sums[::2], sums[1::2])]
        yr_s[n][image] = sums[0]
        each(1, images, lambda t: across(n, t).start())

    def share(n, t):
        q = peer(t)
        spot = ag_refs[n].at[core, chip]
        return remote(spot, spot, as_sem.at[n], ar_sem.at[n], {"band": 2 * q + core})

    def share_bulk(n):
        some = ag_refs[n].at[core, pl.ds(0, 15)]
        return remote(some, some, as_sem.at[n], ar_sem.at[n], partner)

    def share_all(n, t):
        spot = ag_refs[n].at[slot]
        where = {"band": lax.rem(band + t, bands)}
        return remote(spot, spot, as_sem.at[n], ar_sem.at[n], where)

    def share_all_bulk(n):
        some = ag_refs[n].at[pl.ds(0, 31)]
        return remote(some, some, as_sem.at[n], ar_sem.at[n], partner)

    def share_send(n):
        across_bulk(n).wait_recv()
        total = yr_s[n][0]
        for q in range(1, images):
            total = total + yr_s[n][q]
        total = (total * scale).astype(BF)
        if n < 2:
            ag_refs[n][core, chip] = total
            each(1, chips, lambda t: share(n, t).start())
        else:
            ag_refs[n][slot] = total
            each(1, bands, lambda t: share_all(n, t).start())

    def relay(n, side):
        spot = ag_refs[n].at[side]
        return remote(spot, spot, rs_sem.at[n], rr_sem.at[n], partner)

    def relay_send(n):
        share_bulk(n).wait_recv()
        relay(n, core).start()

    def settle(n):
        across_bulk(n).wait_send()
        if n < 2:
            bulk(n).wait_send()
            share_bulk(n).wait_send()
            relay(n, core).wait_send()
        else:
            direct_bulk(n).wait_send()
            share_all_bulk(n).wait_send()

    def widen(v):
        return jnp.concatenate([v, jnp.zeros((D, D - CELLS), F32)], axis=1).astype(BF)

    def own(i):
        spread_grad(i)
        project_own(i)
        attend_own(i, built[i])

    built = [build(0)]
    for load in loads[4:]:
        load.wait()
    vwt_s[...] = vw_s[...].T
    og = og_s[...]
    g_s[...] = dot(ow_s[...], og, 1, 1).astype(BF).astype(F32)
    v_s[1] = widen(dot(vwt_s[...], x, 1, 1))
    for i in range(PAIRS):
        pick_s[i, 2, 2 * TAIL :, :] = jnp.zeros((128 - 2 * TAIL, 128), F32)
    built.append(build(1))
    own(0)

    pl.semaphore_wait(barrier, bands - 1 + images - 1)
    halo_up = remote(x_s, halo_s.at[0], halo_sem.at[0], halo_sem.at[2], up)
    halo_down = remote(x_s, halo_s.at[1], halo_sem.at[1], halo_sem.at[3], down)
    halo_up.start()
    halo_down.start()

    built.append(build(2))
    own(1)
    built.append(build(3))
    own(2)
    own(3)

    halo_up.wait()
    halo_down.wait()

    v_s[0] = widen(dot(vwt_s[...], halo_s[0], 1, 1))
    v_s[2] = widen(dot(vwt_s[...], halo_s[1], 1, 1))
    project_beside(0)
    project_beside(1)
    pair_weights(0, (0, 1))
    swap_send(0)
    project_beside(2)
    project_beside(3)
    pair_weights(1, (2, 3))
    swap_send(1)
    attend_beside(0, built[0])
    plane_send(0)
    plane_send(1)
    attend_beside(1, built[1])
    attend_beside(2, built[2])
    attend_beside(3, built[3])
    weights(2, [dot(lg_s[...], x)])
    direct_send(2)
    send_s[0] = vg_s[0].T
    send_s[1] = vg_s[2].T
    back_down = remote(send_s.at[0], back_s.at[1], back_sem.at[0], back_sem.at[2], down)
    back_up = remote(send_s.at[1], back_s.at[0], back_sem.at[1], back_sem.at[3], up)
    back_down.start()
    back_up.start()
    partial_grad = dot(lg_s[...].astype(F32).T.astype(BF), lw_s[...], 1, 1)
    own_t = own_s[...].T
    across_send(0)
    across_send(1)
    back_down.wait()
    back_up.wait()
    value_grad = own_t + back_s[0].astype(F32) + back_s[1].astype(F32)
    input_grad = dot(value_grad.astype(BF), vwt_s[...]) + partial_grad
    ig_ref[...] = input_grad.astype(BF)
    across_send(2)
    share_send(0)
    share_send(1)
    share_send(2)
    relay_send(0)
    relay_send(1)
    for n in range(2):
        relay(n, 1 - core).wait_recv()
    share_all_bulk(2).wait_recv()
    for n in range(3):
        settle(n)


def finish_kernel(aga_ref, agb_ref, agc_ref, ig_in, ig_ref, gv_ref, gl_ref, go_ref):
    ig_ref[...] = ig_in[...]
    for c in range(2):
        cols = slice(c * 128, (c + 1) * 128)
        a = aga_ref[c].reshape(CHUNKS[0], 128).astype(F32)
        b = agb_ref[c].reshape(CHUNKS[1], 128).astype(F32)
        gv_ref[cols, :128] = a[:128].T
        gv_ref[cols, 128:] = b[:128].T
        go_ref[:128, cols] = a[128:]
        go_ref[128:, cols] = b[128:]
        gl_ref[cols, :] = agc_ref[c * 16 : c * 16 + 16].reshape(CHUNKS[2], 128).astype(F32).T


def body(features, corner_rows, corner_weights, out_grad, vw, lw, ow):
    vm = pl.BlockSpec(memory_space=pltpu.VMEM)
    hbm = pl.BlockSpec(memory_space=pltpu.HBM)
    dma = pltpu.SemaphoreType.DMA
    ig, aga, agb, agc = pl.pallas_call(
        whole_kernel,
        out_shape=(
            pltpu.VMEM((CELLS, D), BF),
            pltpu.VMEM((2, 16, CHUNKS[0] // 16, 128), BF),
            pltpu.VMEM((2, 16, CHUNKS[1] // 16, 128), BF),
            pltpu.VMEM((32, CHUNKS[2] // 16, 128), BF),
        ),
        in_specs=[hbm] * 7,
        out_specs=[vm] * 4,
        scratch_shapes=[
            pltpu.VMEM((CELLS, D), BF),
            pltpu.VMEM((CELLS, D), BF),
            pltpu.VMEM((D, D), BF),
            pltpu.VMEM((D, HEADS * PTS), BF),
            pltpu.VMEM((D, D), BF),
            pltpu.VMEM((HEADS, 64, CELLS), I32),
            pltpu.VMEM((HEADS, 64, CELLS), F32),
            pltpu.VMEM((D, D), BF),
            pltpu.VMEM((2, CELLS, D), BF),
            pltpu.VMEM((3, D, D), BF),
            pltpu.VMEM((HEADS, PTS, CELLS), F32),
            pltpu.VMEM((D, CELLS), F32),
            pltpu.VMEM((D, CELLS), BF),
            pltpu.VMEM((12, 64, 128), F32),
            pltpu.VMEM((D, CELLS), F32),
            pltpu.VMEM((3, D, CELLS), BF),
            pltpu.VMEM((2, 3, 4, 64, 128), F32),
            pltpu.VMEM((PAIRS, 3, PAD, LANES), BF),
            pltpu.VMEM((HEADS * PTS, CELLS), BF),
            pltpu.VMEM((2, CELLS, D), BF),
            pltpu.VMEM((2, CELLS, D), BF),
            pltpu.VMEM((PAIRS, 2 * HEAD, LANES), BF),
            pltpu.VMEM((PAIRS, 3, 128, 2 * HEAD), BF),
            pltpu.VMEM((PAIRS, 2 * HEAD, LANES), F32),
            pltpu.VMEM((PAIRS, 3, 128, 128), I32),
            pltpu.VMEM((PAIRS, 3, 128, 128), F32),
            [pltpu.VMEM((2, n, 128), F32) for n in CHUNKS],
            [pltpu.VMEM((n, 128), BF) for n in CHUNKS[:2]],
            [pltpu.VMEM((n, 128), BF) for n in CHUNKS[:2]],
            [pltpu.VMEM((16, n // 16, 128), BF) for n in CHUNKS[:2]]
            + [pltpu.VMEM((32, n // 16, 128), BF) for n in CHUNKS[2:]],
            [pltpu.VMEM((16, n // 16, 128), BF) for n in CHUNKS[:2]]
            + [pltpu.VMEM((32, n // 16, 128), BF) for n in CHUNKS[2:]],
            [pltpu.VMEM((4, n // 16, 128), F32) for n in CHUNKS],
            dma((9,)),
            dma((4,)),
            dma((4,)),
            dma((2, 2)),
            dma((3,)),
            dma((3,)),
            dma((3,)),
            dma((3,)),
            dma((3,)),
            dma((3,)),
            dma((2,)),
            dma((2,)),
        ],
        compiler_params=pltpu.CompilerParams(
            collective_id=0, has_side_effects=True, vmem_limit_bytes=60 * 10**6
        ),
        name="whole",
    )(
        features[0].T,
        corner_rows[0],
        corner_weights[0],
        out_grad[0].T,
        vw,
        lw,
        ow,
    )
    ig, gv, gl, go = pl.pallas_call(
        finish_kernel,
        out_shape=(
            jax.ShapeDtypeStruct((CELLS, D), BF),
            jax.ShapeDtypeStruct((D, D), F32),
            jax.ShapeDtypeStruct((D, HEADS * PTS), F32),
            jax.ShapeDtypeStruct((D, D), F32),
        ),
        in_specs=[vm] * 4,
        out_specs=[vm] * 4,
        compiler_params=pltpu.CompilerParams(vmem_limit_bytes=8 * 2**20),
        name="finish",
    )(aga, agb, agc, ig)
    return (ig.T[None], gv, gl, go)


def solution(mesh):
    placed = (
        P("dp", None, "band"),
        P("dp", None, None, "band"),
        P("dp", None, None, "band"),
        P("dp", None, "band"),
        P(),
        P(),
        P(),
    )
    return jax.shard_map(
        body,
        mesh=mesh,
        in_specs=placed,
        out_specs=(P("dp", None, "band"), P(), P(), P()),
        check_vma=False,
    )
```

```python
import jax
import jax.numpy as jnp
from jax import lax
from jax.experimental import pallas as pl
from jax.experimental.pallas import tpu as pltpu
from jax.sharding import PartitionSpec as P

HEADS = 8
LEVELS = 4
POINTS = 4
D = 256
CELLS = 172
PAD = 176
TAIL = CELLS - 128
GAP = 128 - 2 * TAIL
LANES = 384
PAIRS = HEADS // 2
SIDE = 4
HEAD = D // HEADS
PTS = LEVELS * POINTS
CHUNKS = (256, 256, 128)
BF = jnp.bfloat16
F32 = jnp.float32
I32 = jnp.int32


def dot(a, b, ca=1, cb=0):
    return lax.dot_general(a, b, (((ca,), (cb,)), ((), ())), preferred_element_type=F32)


def lane_pick(table, index):
    numbers = lax.GatherDimensionNumbers(
        offset_dims=(),
        collapsed_slice_dims=(1,),
        start_index_map=(1,),
        operand_batching_dims=(0,),
        start_indices_batching_dims=(0,),
    )
    return lax.gather(
        table,
        index[..., None],
        numbers,
        slice_sizes=(1, 1),
        mode=lax.GatherScatterMode.PROMISE_IN_BOUNDS,
    )


def whole_kernel(
    x_hbm,
    rows_hbm,
    cw_hbm,
    og_hbm,
    vw_hbm,
    lw_hbm,
    ow_hbm,
    ig_ref,
    aga_ref,
    agb_ref,
    agc_ref,
    x_s,
    og_s,
    vw_s,
    lw_s,
    ow_s,
    rows_s,
    cw_s,
    vwt_s,
    halo_s,
    v_s,
    att_s,
    g_s,
    samp_s,
    rep_s,
    own_s,
    vg_s,
    wide_s,
    m_s,
    lg_s,
    send_s,
    back_s,
    gp_s,
    gt_s,
    half_s,
    at_s,
    pick_s,
    rest_s,
    w_s,
    cs_s,
    cr_s,
    ps_s,
    pr_s,
    yr_s,
    in_sem,
    halo_sem,
    back_sem,
    core_sem,
    ps_sem,
    pr_sem,
    ys_sem,
    yr_sem,
    as_sem,
    ar_sem,
    rs_sem,
    rr_sem,
):
    ag_refs = (aga_ref, agb_ref, agc_ref)
    band = lax.axis_index("band")
    image = lax.axis_index("dp")
    bands = lax.axis_size("band")
    images = lax.axis_size("dp")
    chips = bands // 2
    core = lax.rem(band, 2)
    chip = lax.div(band, 2)
    up = {"band": lax.rem(band + 1, bands)}
    down = {"band": lax.rem(band + bands - 1, bands)}
    partner = {"band": band + 1 - 2 * core}

    row, column = lax.div(chip, SIDE), lax.rem(chip, SIDE)
    steps = [(a, b) for a in range(SIDE) for b in range(SIDE)]
    steps.sort(key=lambda ab: -sum(min(n, SIDE - n) for n in ab))

    def peer(t):
        a, b = steps[t - 1]
        return lax.rem(row + a, SIDE) * SIDE + lax.rem(column + b, SIDE)

    def side(t):
        return core if t % 2 and t + 1 < bands else 1 - core

    def any_peer(t):
        return 2 * peer((t + 1) // 2) + side(t)

    def remote(src, dst, send, recv, where):
        return pltpu.make_async_remote_copy(
            src_ref=src,
            dst_ref=dst,
            send_sem=send,
            recv_sem=recv,
            device_id=where,
            device_id_type=pl.DeviceIdType.MESH,
        )

    def each(low, high, step):
        for t in range(low, high):
            step(t)

    barrier = pltpu.get_barrier_semaphore()

    def greet(where):
        pl.semaphore_signal(barrier, inc=1, device_id=where, device_id_type=pl.DeviceIdType.MESH)

    first, rest = pl.ds(0, 2), pl.ds(2, HEADS - 2)
    loads = [
        pltpu.make_async_copy(src, dst, in_sem.at[n])
        for n, (src, dst) in enumerate(
            [
                (x_hbm, x_s),
                (lw_hbm, lw_s),
                (rows_hbm.at[first], rows_s.at[first]),
                (cw_hbm.at[first], cw_s.at[first]),
                (vw_hbm, vw_s),
                (og_hbm, og_s),
                (ow_hbm, ow_s),
                (rows_hbm.at[rest], rows_s.at[rest]),
                (cw_hbm.at[rest], cw_s.at[rest]),
            ]
        )
    ]
    for load in loads:
        load.start()
    each(1, bands, lambda t: greet({"band": any_peer(t)}))
    each(1, images, lambda t: greet({"dp": lax.rem(image + t, images)}))

    loads[0].wait()
    loads[1].wait()
    x = x_s[...]
    att_s[...] = dot(lw_s[...].T, x, 1, 1).reshape(HEADS, PTS, CELLS)
    loads[2].wait()
    loads[3].wait()

    def packed(first, second):
        tail = jnp.concatenate(
            [first[:, 128:], second[:, 128:], jnp.zeros((first.shape[0], GAP), first.dtype)],
            axis=1,
        )
        return [first[:, :128], second[:, :128], tail]

    sub = lax.broadcasted_iota(I32, (16, 128), 0)
    ids = [(sub + cb * 16).astype(F32).astype(BF) for cb in range(11)]
    base = (band - 1) * CELLS
    nil = jnp.zeros((), BF)

    def build(i):
        cells = packed(rows_s[2 * i] - base, rows_s[2 * i + 1] - base)
        cw = packed(cw_s[2 * i], cw_s[2 * i + 1])
        logit = packed(att_s[2 * i], att_s[2 * i + 1])
        att = []
        for g in range(3):
            e = jnp.exp(logit[g])
            att.append(e / jnp.sum(e, axis=0, keepdims=True))
            rep = rep_s.at[(i % 2) * 6 + g]
            for c in range(4):
                rep[pl.ds(c, PTS, stride=4), :] = att[g]
            over1 = cells[g] >= CELLS
            over2 = cells[g] >= 2 * CELLS
            r = cells[g] - jnp.where(over2, 2 * CELLS, jnp.where(over1, CELLS, 0))
            w = (rep[...] * cw[g]).astype(BF).astype(F32)
            zero = jnp.zeros_like(w)
            wide = wide_s.at[i % 2, g]
            wide[0] = r.astype(F32)
            wide[1] = jnp.where(over1, zero, w)
            wide[2] = jnp.where(over1, jnp.where(over2, zero, w), zero)
            wide[3] = jnp.where(over2, w, zero)
            for cbs, levels in ((range(8), (0,)), (range(8, 10), (1,)), (range(10, 11), (2, 3))):
                acc = [[None] * 3 for _ in cbs]
                for lev in levels:
                    for k in range(lev * 16, lev * 16 + 16):
                        row = [
                            jnp.broadcast_to(wide[n, pl.ds(k, 1), :], (16, 128)).astype(BF)
                            for n in range(4)
                        ]
                        for at, cb in enumerate(cbs):
                            hit = row[0] == ids[cb]
                            for j in range(3):
                                term = jnp.where(hit, row[1 + j], nil)
                                old = acc[at][j]
                                acc[at][j] = term if old is None else old + term
                for at, cb in enumerate(cbs):
                    for j in range(3):
                        m_s[i, j, cb * 16 : cb * 16 + 16, g * 128 : (g + 1) * 128] = acc[at][j]
        return cells, cw, att

    def heads_of(i):
        return slice(i * 2 * HEAD, (i + 1) * 2 * HEAD)

    def parts(at):
        over1 = at >= CELLS
        over2 = at >= 2 * CELLS
        r = at - jnp.where(over2, 2 * CELLS, jnp.where(over1, CELLS, 0))
        return over1, over2, r < 128, jnp.bitwise_and(r, 127)

    def spread_grad(i):
        g0 = g_s[i * 2 * HEAD : i * 2 * HEAD + HEAD, :]
        g1 = g_s[i * 2 * HEAD + HEAD : (i + 1) * 2 * HEAD, :]
        none = jnp.zeros((HEAD, 128), F32)
        top = [
            g0[:, :128],
            none,
            jnp.concatenate([g0[:, 128:], none[:, : 128 - TAIL]], axis=1),
        ]
        bottom = [
            none,
            g1[:, :128],
            jnp.concatenate([none[:, :TAIL], g1[:, 128:], none[:, : 128 - 2 * TAIL]], axis=1),
        ]
        for g in range(3):
            both = jnp.concatenate([top[g], bottom[g]], axis=0)
            gp_s[i, :, g * 128 : (g + 1) * 128] = both.astype(BF)
            gt_s[i, g] = both.T.astype(BF)

    def project_own(i):
        hs = heads_of(i)
        m_j = m_s[i, 1, :CELLS, :]
        half_s[i] = dot(v_s[1, hs, :CELLS], m_j)
        part = dot(gp_s[i], m_j, 1, 1)
        own_s[hs, :] = part
        vg_s[1, hs, :] = part.astype(BF)

    def project_beside(i):
        hs = heads_of(i)
        samp = half_s[i]
        for j in (0, 2):
            m_j = m_s[i, j, :CELLS, :]
            samp = samp + dot(v_s[j, hs, :CELLS], m_j)
            vg_s[j, hs, :] = dot(gp_s[i], m_j, 1, 1).astype(BF)
        s0 = jnp.concatenate([samp[:HEAD, :128], samp[:HEAD, 256 : 256 + TAIL]], axis=1)
        s1 = jnp.concatenate(
            [samp[HEAD:, 128:256], samp[HEAD:, 256 + TAIL : 256 + 2 * TAIL]], axis=1
        )
        samp_s[hs, :] = jnp.concatenate([s0, s1], axis=0).astype(BF)

    def lookup(table, near, index):
        near_part = lane_pick(table[:, :128], index)
        return jnp.where(near, near_part, lane_pick(table[:, 128:], index))

    def groups(g):
        return range(0, 128 if g < 2 else 2 * TAIL, 8)

    def attend_own(i, built):
        for g in range(3):
            at = jnp.concatenate([built[0][g], jnp.zeros((64, 128), I32)], axis=0).T
            at_s[i, g] = at
            score = dot(gt_s[i, g], v_s[1, heads_of(i), :])
            for q in groups(g):
                _, _, near, index = parts(at[q : q + 8])
                pick_s[i, g, q : q + 8, :] = lookup(score[q : q + 8], near, index)

    def attend_beside(i, built):
        _, cw, att = built
        lgs = []
        for g in range(3):
            below = dot(gt_s[i, g], v_s[0, heads_of(i), :128])
            above = dot(gt_s[i, g], v_s[2, heads_of(i), :128])
            rest = dot(gt_s[i, g], rest_s[heads_of(i), :])
            for q in groups(g):
                qs = slice(q, q + 8)
                over1, over2, near, index = parts(at_s[i, g, qs, :])
                index = jnp.where(near, index, jnp.where(over2, index + TAIL, index))
                pick = jnp.where(over2, lane_pick(above[qs], index), lane_pick(below[qs], index))
                pick = jnp.where(near, pick, lane_pick(rest[qs], index))
                mine = jnp.where(over2, pick, pick_s[i, g, qs, :])
                pick_s[i, g, qs, :] = jnp.where(over1, mine, pick)
            rep = rep_s.at[(i % 2) * 6 + 3 + g]
            rep[...] = pick_s[i, g, :, :64].T * cw[g]
            ag = jnp.zeros((PTS, 128), F32)
            for c in range(4):
                ag = ag + rep[pl.ds(c, PTS, stride=4), :]
            lgs.append(att[g] * (ag - jnp.sum(att[g] * ag, axis=0, keepdims=True)))
        l0 = jnp.concatenate([lgs[0], lgs[2][:, :TAIL]], axis=1)
        l1 = jnp.concatenate([lgs[1], lgs[2][:, TAIL : 2 * TAIL]], axis=1)
        lg_s[i * 2 * PTS : (i + 1) * 2 * PTS, :] = jnp.concatenate([l0, l1], axis=0).astype(BF)

    scale = 1.0 / float(images * bands * CELLS) ** 0.5

    def weights(n, blocks):
        for c in range(2):
            at = 0
            for block in blocks:
                w_s[n][c, at : at + block.shape[0], :] = block[:, c * 128 : (c + 1) * 128]
                at += block.shape[0]

    def pair_weights(n, pairs):
        first, last = pairs[0] * 2 * HEAD, (pairs[-1] + 1) * 2 * HEAD
        gv = dot(vg_s[0, first:last, :], halo_s[0])
        gv = gv + dot(vg_s[1, first:last, :], x)
        gv = gv + dot(vg_s[2, first:last, :], halo_s[1])
        weights(n, [gv, dot(samp_s[first:last, :], og)])

    def swap(n):
        return remote(cs_s[n], cr_s[n], core_sem.at[n, 0], core_sem.at[n, 1], partner)

    def swap_send(n):
        cs_s[n][...] = w_s[n][1 - core].astype(BF)
        swap(n).start()

    def piece(n, t, where):
        q = peer(t)
        return remote(
            ps_s[n].at[q], pr_s[n].at[chip], ps_sem.at[n], pr_sem.at[n], {"band": 2 * q + core}
        )

    def plane_send(n):
        swap(n).wait()
        half = w_s[n][core] + cr_s[n][...].astype(F32)
        ps_s[n][...] = half.astype(BF).reshape(ps_s[n].shape)
        each(1, chips, lambda t: piece(n, t, None).start())
        pr_s[n][chip] = ps_s[n][chip]

    def bulk(n):
        some = pl.ds(0, 15)
        return remote(
            ps_s[n].at[some], pr_s[n].at[some], ps_sem.at[n], pr_sem.at[n], partner
        )

    def across(n, t):
        q = lax.rem(image + t, images)
        spot = yr_s[n].at[image]
        return remote(spot, spot, ys_sem.at[n], yr_sem.at[n], {"dp": q})

    def across_bulk(n):
        some = yr_s[n].at[pl.ds(0, 3)]
        return remote(some, some, ys_sem.at[n], yr_sem.at[n], partner)

    slot = core * 16 + chip

    def direct(n, t):
        q = any_peer(t)
        return remote(
            ps_s[n].at[side(t) * 16 + peer((t + 1) // 2)],
            pr_s[n].at[slot],
            ps_sem.at[n],
            pr_sem.at[n],
            {"band": q},
        )

    def direct_bulk(n):
        some = pl.ds(0, 31)
        return remote(
            ps_s[n].at[some], pr_s[n].at[some], ps_sem.at[n], pr_sem.at[n], partner
        )

    def direct_send(n):
        ps_s[n][...] = w_s[n][...].astype(BF).reshape(ps_s[n].shape)
        each(1, bands, lambda t: direct(n, t).start())
        pr_s[n][slot] = ps_s[n][slot]

    def across_send(n):
        pieces = []
        if n < 2:
            bulk(n).wait_recv()
            pieces = [pr_s[n][q] for q in range(16)]
        else:
            direct_bulk(n).wait_recv()
            pieces = [pr_s[n][q] for q in range(32)]
        sums = [piece.astype(F32) for piece in pieces]
        while len(sums) > 1:
            sums = [a + b for a, b in zip(sums[::2], sums[1::2])]
        yr_s[n][image] = sums[0]
        each(1, images, lambda t: across(n, t).start())

    def share(n, t):
        q = peer(t)
        spot = ag_refs[n].at[core, chip]
        return remote(spot, spot, as_sem.at[n], ar_sem.at[n], {"band": 2 * q + core})

    def share_bulk(n):
        some = ag_refs[n].at[core, pl.ds(0, 15)]
        return remote(some, some, as_sem.at[n], ar_sem.at[n], partner)

    def share_all(n, t):
        spot = ag_refs[n].at[slot]
        where = {"band": any_peer(t)}
        return remote(spot, spot, as_sem.at[n], ar_sem.at[n], where)

    def share_all_bulk(n):
        some = ag_refs[n].at[pl.ds(0, 31)]
        return remote(some, some, as_sem.at[n], ar_sem.at[n], partner)

    def share_send(n):
        across_bulk(n).wait_recv()
        total = yr_s[n][0]
        for q in range(1, images):
            total = total + yr_s[n][q]
        total = (total * scale).astype(BF)
        if n < 1:
            ag_refs[n][core, chip] = total
            each(1, chips, lambda t: share(n, t).start())
        else:
            ag_refs[n][slot] = total
            each(1, bands, lambda t: share_all(n, t).start())

    def relay(n, side):
        spot = ag_refs[n].at[side]
        return remote(spot, spot, rs_sem.at[n], rr_sem.at[n], partner)

    def relay_send(n):
        share_bulk(n).wait_recv()
        relay(n, core).start()

    def settle(n):
        across_bulk(n).wait_send()
        (bulk if n < 2 else direct_bulk)(n).wait_send()
        if n < 1:
            share_bulk(n).wait_send()
            relay(n, core).wait_send()
        else:
            share_all_bulk(n).wait_send()

    def widen(v):
        return jnp.concatenate([v, jnp.zeros((D, D - CELLS), F32)], axis=1).astype(BF)

    def own(i):
        spread_grad(i)
        project_own(i)
        attend_own(i, built[i])

    built = [build(0)]
    for load in loads[4:]:
        load.wait()
    vwt_s[...] = vw_s[...].T
    og = og_s[...]
    g_s[...] = dot(ow_s[...], og, 1, 1).astype(BF).astype(F32)
    v_s[1] = widen(dot(vwt_s[...], x, 1, 1))
    for i in range(PAIRS):
        pick_s[i, 2, 2 * TAIL :, :] = jnp.zeros((128 - 2 * TAIL, 128), F32)
    built.append(build(1))
    own(0)

    pl.semaphore_wait(barrier, bands - 1 + images - 1)
    halo_up = remote(x_s, halo_s.at[0], halo_sem.at[0], halo_sem.at[2], up)
    halo_down = remote(x_s, halo_s.at[1], halo_sem.at[1], halo_sem.at[3], down)
    halo_up.start()
    halo_down.start()

    built.append(build(2))
    own(1)
    built.append(build(3))
    own(2)
    own(3)

    halo_up.wait()
    halo_down.wait()

    low = dot(vwt_s[...], halo_s[0], 1, 1)
    high = dot(vwt_s[...], halo_s[1], 1, 1)
    v_s[0] = widen(low)
    v_s[2] = widen(high)
    rest_s[...] = jnp.concatenate(
        [low[:, 128:], high[:, 128:], jnp.zeros((D, GAP), F32)], axis=1
    ).astype(BF)
    project_beside(0)
    project_beside(1)
    pair_weights(0, (0, 1))
    swap_send(0)
    project_beside(2)
    project_beside(3)
    pair_weights(1, (2, 3))
    swap_send(1)
    attend_beside(0, built[0])
    attend_beside(1, built[1])
    plane_send(0)
    plane_send(1)
    attend_beside(2, built[2])
    attend_beside(3, built[3])
    weights(2, [dot(lg_s[...], x)])
    direct_send(2)
    send_s[0] = vg_s[0].T
    send_s[1] = vg_s[2].T
    back_down = remote(send_s.at[0], back_s.at[1], back_sem.at[0], back_sem.at[2], down)
    back_up = remote(send_s.at[1], back_s.at[0], back_sem.at[1], back_sem.at[3], up)
    back_down.start()
    back_up.start()
    partial_grad = dot(lg_s[...].astype(F32).T.astype(BF), lw_s[...], 1, 1)
    own_t = own_s[...].T
    across_send(0)
    across_send(1)
    back_down.wait()
    back_up.wait()
    value_grad = own_t + back_s[0].astype(F32) + back_s[1].astype(F32)
    input_grad = dot(value_grad.astype(BF), vwt_s[...]) + partial_grad
    ig_ref[...] = input_grad.astype(BF)
    across_send(2)
    share_send(0)
    share_send(1)
    share_send(2)
    relay_send(0)
    share_all_bulk(1).wait_recv()
    share_all_bulk(2).wait_recv()
    relay(0, 1 - core).wait_recv()
    for n in range(3):
        settle(n)


def finish_kernel(
    aga_ref, agb_ref, agc_ref, ig_in, ig_hbm, gv_hbm, gl_hbm, go_hbm, gv_s, gl_s, go_s, sem
):
    copies = [
        pltpu.make_async_copy(src, dst, sem.at[n])
        for n, (src, dst) in enumerate(
            [
                (ig_in, ig_hbm),
                (go_s, go_hbm),
                (gv_s.at[:128], gv_hbm.at[:128]),
                (gv_s.at[128:], gv_hbm.at[128:]),
                (gl_s, gl_hbm),
            ]
        )
    ]
    copies[0].start()
    parts = [
        (
            aga_ref[c].reshape(CHUNKS[0], 128).astype(F32),
            agb_ref[c * 16 : c * 16 + 16].reshape(CHUNKS[1], 128).astype(F32),
        )
        for c in range(2)
    ]
    for c, (a, b) in enumerate(parts):
        cols = slice(c * 128, (c + 1) * 128)
        go_s[:128, cols] = a[128:]
        go_s[128:, cols] = b[128:]
    copies[1].start()
    for c, (a, b) in enumerate(parts):
        cols = slice(c * 128, (c + 1) * 128)
        gv_s[cols, :128] = a[:128].T
        gv_s[cols, 128:] = b[:128].T
        copies[2 + c].start()
    for c in range(2):
        cols = slice(c * 128, (c + 1) * 128)
        gl_s[cols, :] = agc_ref[c * 16 : c * 16 + 16].reshape(CHUNKS[2], 128).astype(F32).T
    copies[4].start()
    for copy in copies:
        copy.wait()


def body(features, corner_rows, corner_weights, out_grad, vw, lw, ow):
    vm = pl.BlockSpec(memory_space=pltpu.VMEM)
    hbm = pl.BlockSpec(memory_space=pltpu.HBM)
    dma = pltpu.SemaphoreType.DMA
    ig, aga, agb, agc = pl.pallas_call(
        whole_kernel,
        out_shape=(
            pltpu.VMEM((CELLS, D), BF),
            pltpu.VMEM((2, 16, CHUNKS[0] // 16, 128), BF),
            pltpu.VMEM((32, CHUNKS[1] // 16, 128), BF),
            pltpu.VMEM((32, CHUNKS[2] // 16, 128), BF),
        ),
        in_specs=[hbm] * 7,
        out_specs=[vm] * 4,
        scratch_shapes=[
            pltpu.VMEM((CELLS, D), BF),
            pltpu.VMEM((CELLS, D), BF),
            pltpu.VMEM((D, D), BF),
            pltpu.VMEM((D, HEADS * PTS), BF),
            pltpu.VMEM((D, D), BF),
            pltpu.VMEM((HEADS, 64, CELLS), I32),
            pltpu.VMEM((HEADS, 64, CELLS), F32),
            pltpu.VMEM((D, D), BF),
            pltpu.VMEM((2, CELLS, D), BF),
            pltpu.VMEM((3, D, D), BF),
            pltpu.VMEM((HEADS, PTS, CELLS), F32),
            pltpu.VMEM((D, CELLS), F32),
            pltpu.VMEM((D, CELLS), BF),
            pltpu.VMEM((12, 64, 128), F32),
            pltpu.VMEM((D, CELLS), F32),
            pltpu.VMEM((3, D, CELLS), BF),
            pltpu.VMEM((2, 3, 4, 64, 128), F32),
            pltpu.VMEM((PAIRS, 3, PAD, LANES), BF),
            pltpu.VMEM((HEADS * PTS, CELLS), BF),
            pltpu.VMEM((2, CELLS, D), BF),
            pltpu.VMEM((2, CELLS, D), BF),
            pltpu.VMEM((PAIRS, 2 * HEAD, LANES), BF),
            pltpu.VMEM((PAIRS, 3, 128, 2 * HEAD), BF),
            pltpu.VMEM((PAIRS, 2 * HEAD, LANES), F32),
            pltpu.VMEM((PAIRS, 3, 128, 128), I32),
            pltpu.VMEM((PAIRS, 3, 128, 128), F32),
            pltpu.VMEM((D, 128), BF),
            [pltpu.VMEM((2, n, 128), F32) for n in CHUNKS],
            [pltpu.VMEM((n, 128), BF) for n in CHUNKS[:2]],
            [pltpu.VMEM((n, 128), BF) for n in CHUNKS[:2]],
            [pltpu.VMEM((16, n // 16, 128), BF) for n in CHUNKS[:2]]
            + [pltpu.VMEM((32, n // 16, 128), BF) for n in CHUNKS[2:]],
            [pltpu.VMEM((16, n // 16, 128), BF) for n in CHUNKS[:2]]
            + [pltpu.VMEM((32, n // 16, 128), BF) for n in CHUNKS[2:]],
            [pltpu.VMEM((4, n // 16, 128), F32) for n in CHUNKS],
            dma((9,)),
            dma((4,)),
            dma((4,)),
            dma((2, 2)),
            dma((3,)),
            dma((3,)),
            dma((3,)),
            dma((3,)),
            dma((3,)),
            dma((3,)),
            dma((1,)),
            dma((1,)),
        ],
        compiler_params=pltpu.CompilerParams(
            collective_id=0, has_side_effects=True, vmem_limit_bytes=60 * 10**6
        ),
        name="whole",
    )(
        features[0].T,
        corner_rows[0],
        corner_weights[0],
        out_grad[0].T,
        vw,
        lw,
        ow,
    )
    ig, gv, gl, go = pl.pallas_call(
        finish_kernel,
        out_shape=(
            jax.ShapeDtypeStruct((CELLS, D), BF),
            jax.ShapeDtypeStruct((D, D), F32),
            jax.ShapeDtypeStruct((D, HEADS * PTS), F32),
            jax.ShapeDtypeStruct((D, D), F32),
        ),
        in_specs=[vm] * 4,
        out_specs=[hbm] * 4,
        scratch_shapes=[
            pltpu.VMEM((D, D), F32),
            pltpu.VMEM((D, HEADS * PTS), F32),
            pltpu.VMEM((D, D), F32),
            dma((5,)),
        ],
        compiler_params=pltpu.CompilerParams(vmem_limit_bytes=8 * 2**20),
        name="finish",
    )(aga, agb, agc, ig)
    return (ig.T[None], gv, gl, go)


def solution(mesh):
    placed = (
        P("dp", None, "band"),
        P("dp", None, None, "band"),
        P("dp", None, None, "band"),
        P("dp", None, "band"),
        P(),
        P(),
        P(),
    )
    return jax.shard_map(
        body,
        mesh=mesh,
        in_specs=placed,
        out_specs=(P("dp", None, "band"), P(), P(), P()),
        check_vma=False,
    )
```

```python
import jax
import jax.numpy as jnp
from jax import lax
from jax.experimental import pallas as pl
from jax.experimental.pallas import tpu as pltpu
from jax.sharding import PartitionSpec as P

HEADS = 8
LEVELS = 4
POINTS = 4
D = 256
CELLS = 172
PAD = 176
TAIL = CELLS - 128
GAP = 128 - 2 * TAIL
LANES = 384
PAIRS = HEADS // 2
SIDE = 4
HEAD = D // HEADS
PTS = LEVELS * POINTS
CHUNKS = (256, 256, 128)
BF = jnp.bfloat16
F32 = jnp.float32
I32 = jnp.int32


def dot(a, b, ca=1, cb=0):
    return lax.dot_general(a, b, (((ca,), (cb,)), ((), ())), preferred_element_type=F32)


def lane_pick(table, index):
    numbers = lax.GatherDimensionNumbers(
        offset_dims=(),
        collapsed_slice_dims=(1,),
        start_index_map=(1,),
        operand_batching_dims=(0,),
        start_indices_batching_dims=(0,),
    )
    return lax.gather(
        table,
        index[..., None],
        numbers,
        slice_sizes=(1, 1),
        mode=lax.GatherScatterMode.PROMISE_IN_BOUNDS,
    )


def whole_kernel(
    x_hbm,
    rows_hbm,
    cw_hbm,
    og_hbm,
    vw_hbm,
    lw_hbm,
    ow_hbm,
    ig_ref,
    aga_ref,
    agb_ref,
    agc_ref,
    x_s,
    og_s,
    vw_s,
    lw_s,
    ow_s,
    rows_s,
    cw_s,
    vwt_s,
    halo_s,
    v_s,
    att_s,
    g_s,
    samp_s,
    rep_s,
    own_s,
    vg_s,
    wide_s,
    m_s,
    lg_s,
    send_s,
    back_s,
    gp_s,
    gt_s,
    half_s,
    at_s,
    pick_s,
    rest_s,
    w_s,
    cs_s,
    cr_s,
    ps_s,
    pr_s,
    yr_s,
    in_sem,
    halo_sem,
    back_sem,
    core_sem,
    ps_sem,
    pr_sem,
    ys_sem,
    yr_sem,
    as_sem,
    ar_sem,
    rs_sem,
    rr_sem,
):
    ag_refs = (aga_ref, agb_ref, agc_ref)
    band = lax.axis_index("band")
    image = lax.axis_index("dp")
    bands = lax.axis_size("band")
    images = lax.axis_size("dp")
    chips = bands // 2
    core = lax.rem(band, 2)
    chip = lax.div(band, 2)
    up = {"band": lax.rem(band + 1, bands)}
    down = {"band": lax.rem(band + bands - 1, bands)}
    partner = {"band": band + 1 - 2 * core}

    row, column = lax.div(chip, SIDE), lax.rem(chip, SIDE)
    steps = [(a, b) for a in range(SIDE) for b in range(SIDE)]
    steps.sort(key=lambda ab: -sum(min(n, SIDE - n) for n in ab))

    def peer(t):
        a, b = steps[t - 1]
        return lax.rem(row + a, SIDE) * SIDE + lax.rem(column + b, SIDE)

    def side(t):
        return core if t % 2 and t + 1 < bands else 1 - core

    def any_peer(t):
        return 2 * peer((t + 1) // 2) + side(t)

    def remote(src, dst, send, recv, where):
        return pltpu.make_async_remote_copy(
            src_ref=src,
            dst_ref=dst,
            send_sem=send,
            recv_sem=recv,
            device_id=where,
            device_id_type=pl.DeviceIdType.MESH,
        )

    def each(low, high, step):
        for t in range(low, high):
            step(t)

    barrier = pltpu.get_barrier_semaphore()

    def greet(where):
        pl.semaphore_signal(barrier, inc=1, device_id=where, device_id_type=pl.DeviceIdType.MESH)

    first, rest = pl.ds(0, 2), pl.ds(2, HEADS - 2)
    loads = [
        pltpu.make_async_copy(src, dst, in_sem.at[n])
        for n, (src, dst) in enumerate(
            [
                (x_hbm, x_s),
                (lw_hbm, lw_s),
                (rows_hbm.at[first], rows_s.at[first]),
                (cw_hbm.at[first], cw_s.at[first]),
                (vw_hbm, vw_s),
                (og_hbm, og_s),
                (ow_hbm, ow_s),
                (rows_hbm.at[rest], rows_s.at[rest]),
                (cw_hbm.at[rest], cw_s.at[rest]),
            ]
        )
    ]
    for load in loads:
        load.start()
    each(1, bands, lambda t: greet({"band": any_peer(t)}))
    each(1, images, lambda t: greet({"dp": lax.rem(image + t, images)}))

    loads[0].wait()
    loads[1].wait()
    x = x_s[...]
    att_s[...] = dot(lw_s[...].T, x, 1, 1).reshape(HEADS, PTS, CELLS)
    loads[2].wait()
    loads[3].wait()

    def packed(first, second):
        tail = jnp.concatenate(
            [first[:, 128:], second[:, 128:], jnp.zeros((first.shape[0], GAP), first.dtype)],
            axis=1,
        )
        return [first[:, :128], second[:, :128], tail]

    sub = lax.broadcasted_iota(I32, (16, 128), 0)
    ids = [(sub + cb * 16).astype(F32).astype(BF) for cb in range(11)]
    base = (band - 1) * CELLS
    nil = jnp.zeros((), BF)

    def build(i):
        cells = packed(rows_s[2 * i] - base, rows_s[2 * i + 1] - base)
        cw = packed(cw_s[2 * i], cw_s[2 * i + 1])
        logit = packed(att_s[2 * i], att_s[2 * i + 1])
        att = []
        for g in range(3):
            e = jnp.exp(logit[g])
            att.append(e / jnp.sum(e, axis=0, keepdims=True))
            rep = rep_s.at[(i % 2) * 6 + g]
            for c in range(4):
                rep[pl.ds(c, PTS, stride=4), :] = att[g]
            over1 = cells[g] >= CELLS
            over2 = cells[g] >= 2 * CELLS
            r = cells[g] - jnp.where(over2, 2 * CELLS, jnp.where(over1, CELLS, 0))
            w = (rep[...] * cw[g]).astype(BF).astype(F32)
            zero = jnp.zeros_like(w)
            wide = wide_s.at[i % 2, g]
            wide[0] = r.astype(F32)
            wide[1] = jnp.where(over1, zero, w)
            wide[2] = jnp.where(over1, jnp.where(over2, zero, w), zero)
            wide[3] = jnp.where(over2, w, zero)
            for cbs, levels in ((range(8), (0,)), (range(8, 10), (1,)), (range(10, 11), (2, 3))):
                acc = [[None] * 3 for _ in cbs]
                for lev in levels:
                    for k in range(lev * 16, lev * 16 + 16):
                        row = [
                            jnp.broadcast_to(wide[n, pl.ds(k, 1), :], (16, 128)).astype(BF)
                            for n in range(4)
                        ]
                        for at, cb in enumerate(cbs):
                            hit = row[0] == ids[cb]
                            for j in range(3):
                                term = jnp.where(hit, row[1 + j], nil)
                                old = acc[at][j]
                                acc[at][j] = term if old is None else old + term
                for at, cb in enumerate(cbs):
                    for j in range(3):
                        m_s[i, j, cb * 16 : cb * 16 + 16, g * 128 : (g + 1) * 128] = acc[at][j]
        return cells, cw, att

    def heads_of(i):
        return slice(i * 2 * HEAD, (i + 1) * 2 * HEAD)

    def parts(at):
        over1 = at >= CELLS
        over2 = at >= 2 * CELLS
        r = at - jnp.where(over2, 2 * CELLS, jnp.where(over1, CELLS, 0))
        return over1, over2, r < 128, jnp.bitwise_and(r, 127)

    def spread_grad(i):
        g0 = g_s[i * 2 * HEAD : i * 2 * HEAD + HEAD, :]
        g1 = g_s[i * 2 * HEAD + HEAD : (i + 1) * 2 * HEAD, :]
        none = jnp.zeros((HEAD, 128), F32)
        top = [
            g0[:, :128],
            none,
            jnp.concatenate([g0[:, 128:], none[:, : 128 - TAIL]], axis=1),
        ]
        bottom = [
            none,
            g1[:, :128],
            jnp.concatenate([none[:, :TAIL], g1[:, 128:], none[:, : 128 - 2 * TAIL]], axis=1),
        ]
        for g in range(3):
            both = jnp.concatenate([top[g], bottom[g]], axis=0)
            gp_s[i, :, g * 128 : (g + 1) * 128] = both.astype(BF)
            gt_s[i, g] = both.T.astype(BF)

    def project_own(i):
        hs = heads_of(i)
        half_s[i] = dot(v_s[1, hs, :CELLS], m_s[i, 1, :CELLS, :])
        for j in range(3):
            part = dot(gp_s[i], m_s[i, j, :CELLS, :], 1, 1)
            if j == 1:
                own_s[hs, :] = part
            vg_s[j, hs, :] = part.astype(BF)

    def project_beside(i):
        hs = heads_of(i)
        samp = half_s[i]
        for j in (0, 2):
            samp = samp + dot(v_s[j, hs, :CELLS], m_s[i, j, :CELLS, :])
        s0 = jnp.concatenate([samp[:HEAD, :128], samp[:HEAD, 256 : 256 + TAIL]], axis=1)
        s1 = jnp.concatenate(
            [samp[HEAD:, 128:256], samp[HEAD:, 256 + TAIL : 256 + 2 * TAIL]], axis=1
        )
        samp_s[hs, :] = jnp.concatenate([s0, s1], axis=0).astype(BF)

    def lookup(table, near, index):
        near_part = lane_pick(table[:, :128], index)
        return jnp.where(near, near_part, lane_pick(table[:, 128:], index))

    def groups(g):
        return range(0, 128 if g < 2 else 2 * TAIL, 8)

    def attend_own(i, built):
        for g in range(3):
            at = jnp.concatenate([built[0][g], jnp.zeros((64, 128), I32)], axis=0).T
            at_s[i, g] = at
            score = dot(gt_s[i, g], v_s[1, heads_of(i), :])
            for q in groups(g):
                _, _, near, index = parts(at[q : q + 8])
                pick_s[i, g, q : q + 8, :] = lookup(score[q : q + 8], near, index)

    def attend_beside(i, built):
        _, cw, att = built
        lgs = []
        for g in range(3):
            below = dot(gt_s[i, g], v_s[0, heads_of(i), :128])
            above = dot(gt_s[i, g], v_s[2, heads_of(i), :128])
            rest = dot(gt_s[i, g], rest_s[heads_of(i), :])
            for q in groups(g):
                qs = slice(q, q + 8)
                over1, over2, near, index = parts(at_s[i, g, qs, :])
                index = jnp.where(near, index, jnp.where(over2, index + TAIL, index))
                pick = jnp.where(over2, lane_pick(above[qs], index), lane_pick(below[qs], index))
                pick = jnp.where(near, pick, lane_pick(rest[qs], index))
                mine = jnp.where(over2, pick, pick_s[i, g, qs, :])
                pick_s[i, g, qs, :] = jnp.where(over1, mine, pick)
            rep = rep_s.at[(i % 2) * 6 + 3 + g]
            rep[...] = pick_s[i, g, :, :64].T * cw[g]
            ag = jnp.zeros((PTS, 128), F32)
            for c in range(4):
                ag = ag + rep[pl.ds(c, PTS, stride=4), :]
            lgs.append(att[g] * (ag - jnp.sum(att[g] * ag, axis=0, keepdims=True)))
        l0 = jnp.concatenate([lgs[0], lgs[2][:, :TAIL]], axis=1)
        l1 = jnp.concatenate([lgs[1], lgs[2][:, TAIL : 2 * TAIL]], axis=1)
        lg_s[i * 2 * PTS : (i + 1) * 2 * PTS, :] = jnp.concatenate([l0, l1], axis=0).astype(BF)

    scale = 1.0 / float(images * bands * CELLS) ** 0.5

    def weights(n, blocks):
        for c in range(2):
            at = 0
            for block in blocks:
                w_s[n][c, at : at + block.shape[0], :] = block[:, c * 128 : (c + 1) * 128]
                at += block.shape[0]

    def pair_weights(n, pairs):
        first, last = pairs[0] * 2 * HEAD, (pairs[-1] + 1) * 2 * HEAD
        gv = dot(vg_s[0, first:last, :], halo_s[0])
        gv = gv + dot(vg_s[1, first:last, :], x)
        gv = gv + dot(vg_s[2, first:last, :], halo_s[1])
        weights(n, [gv, dot(samp_s[first:last, :], og)])

    def swap(n):
        return remote(cs_s[n], cr_s[n], core_sem.at[n, 0], core_sem.at[n, 1], partner)

    def swap_send(n):
        cs_s[n][...] = w_s[n][1 - core].astype(BF)
        swap(n).start()

    def piece(n, t, where):
        q = peer(t)
        return remote(
            ps_s[n].at[q], pr_s[n].at[chip], ps_sem.at[n], pr_sem.at[n], {"band": 2 * q + core}
        )

    def plane_send(n):
        swap(n).wait()
        half = w_s[n][core] + cr_s[n][...].astype(F32)
        ps_s[n][...] = half.astype(BF).reshape(ps_s[n].shape)
        each(1, chips, lambda t: piece(n, t, None).start())
        pr_s[n][chip] = ps_s[n][chip]

    def bulk(n):
        some = pl.ds(0, 15)
        return remote(
            ps_s[n].at[some], pr_s[n].at[some], ps_sem.at[n], pr_sem.at[n], partner
        )

    def across(n, t):
        q = lax.rem(image + t, images)
        spot = yr_s[n].at[image]
        return remote(spot, spot, ys_sem.at[n], yr_sem.at[n], {"dp": q})

    def across_bulk(n):
        some = yr_s[n].at[pl.ds(0, 3)]
        return remote(some, some, ys_sem.at[n], yr_sem.at[n], partner)

    slot = core * 16 + chip

    def direct(n, t):
        q = any_peer(t)
        return remote(
            ps_s[n].at[side(t) * 16 + peer((t + 1) // 2)],
            pr_s[n].at[slot],
            ps_sem.at[n],
            pr_sem.at[n],
            {"band": q},
        )

    def direct_bulk(n):
        some = pl.ds(0, 31)
        return remote(
            ps_s[n].at[some], pr_s[n].at[some], ps_sem.at[n], pr_sem.at[n], partner
        )

    def direct_send(n):
        ps_s[n][...] = w_s[n][...].astype(BF).reshape(ps_s[n].shape)
        each(1, bands, lambda t: direct(n, t).start())
        pr_s[n][slot] = ps_s[n][slot]

    def across_send(n):
        pieces = []
        if n < 1:
            bulk(n).wait_recv()
            pieces = [pr_s[n][q] for q in range(16)]
        else:
            direct_bulk(n).wait_recv()
            pieces = [pr_s[n][q] for q in range(32)]
        sums = [piece.astype(F32) for piece in pieces]
        while len(sums) > 1:
            sums = [a + b for a, b in zip(sums[::2], sums[1::2])]
        yr_s[n][image] = sums[0]
        each(0, images - 1, lambda t: across(n, (2, 1, 3)[t]).start())

    def share(n, t):
        q = peer(t)
        spot = ag_refs[n].at[core, chip]
        return remote(spot, spot, as_sem.at[n], ar_sem.at[n], {"band": 2 * q + core})

    def share_bulk(n):
        some = ag_refs[n].at[core, pl.ds(0, 15)]
        return remote(some, some, as_sem.at[n], ar_sem.at[n], partner)

    def share_all(n, t):
        spot = ag_refs[n].at[slot]
        where = {"band": any_peer(t)}
        return remote(spot, spot, as_sem.at[n], ar_sem.at[n], where)

    def share_all_bulk(n):
        some = ag_refs[n].at[pl.ds(0, 31)]
        return remote(some, some, as_sem.at[n], ar_sem.at[n], partner)

    def share_send(n):
        across_bulk(n).wait_recv()
        total = yr_s[n][0]
        for q in range(1, images):
            total = total + yr_s[n][q]
        total = (total * scale).astype(BF)
        if n < 1:
            ag_refs[n][core, chip] = total
            each(1, chips, lambda t: share(n, t).start())
        else:
            ag_refs[n][slot] = total
            each(1, bands, lambda t: share_all(n, t).start())

    def relay(n, side):
        spot = ag_refs[n].at[side]
        return remote(spot, spot, rs_sem.at[n], rr_sem.at[n], partner)

    def relay_send(n):
        share_bulk(n).wait_recv()
        relay(n, core).start()

    def settle(n):
        across_bulk(n).wait_send()
        (bulk if n < 1 else direct_bulk)(n).wait_send()
        if n < 1:
            share_bulk(n).wait_send()
            relay(n, core).wait_send()
        else:
            share_all_bulk(n).wait_send()

    def widen(v):
        return jnp.concatenate([v, jnp.zeros((D, D - CELLS), F32)], axis=1).astype(BF)

    def own(i):
        spread_grad(i)
        project_own(i)
        attend_own(i, built[i])

    built = [build(0)]
    for load in loads[4:]:
        load.wait()
    vwt_s[...] = vw_s[...].T
    og = og_s[...]
    g_s[...] = dot(ow_s[...], og, 1, 1).astype(BF).astype(F32)
    v_s[1] = widen(dot(vwt_s[...], x, 1, 1))
    for i in range(PAIRS):
        pick_s[i, 2, 2 * TAIL :, :] = jnp.zeros((128 - 2 * TAIL, 128), F32)
    built.append(build(1))
    own(0)

    pl.semaphore_wait(barrier, bands - 1 + images - 1)
    halo_up = remote(x_s, halo_s.at[0], halo_sem.at[0], halo_sem.at[2], up)
    halo_down = remote(x_s, halo_s.at[1], halo_sem.at[1], halo_sem.at[3], down)
    halo_up.start()
    halo_down.start()

    built.append(build(2))
    own(1)
    built.append(build(3))
    own(2)
    own(3)

    send_s[0] = vg_s[0].T
    send_s[1] = vg_s[2].T
    back_down = remote(send_s.at[0], back_s.at[1], back_sem.at[0], back_sem.at[2], down)
    back_up = remote(send_s.at[1], back_s.at[0], back_sem.at[1], back_sem.at[3], up)
    back_down.start()
    back_up.start()
    halo_up.wait()
    halo_down.wait()

    low = dot(vwt_s[...], halo_s[0], 1, 1)
    high = dot(vwt_s[...], halo_s[1], 1, 1)
    v_s[0] = widen(low)
    v_s[2] = widen(high)
    rest_s[...] = jnp.concatenate(
        [low[:, 128:], high[:, 128:], jnp.zeros((D, GAP), F32)], axis=1
    ).astype(BF)
    for i in range(PAIRS):
        project_beside(i)
    pair_weights(0, (0, 1))
    pair_weights(1, (2, 3))
    swap_send(0)
    direct_send(1)
    attend_beside(0, built[0])
    attend_beside(1, built[1])
    plane_send(0)
    attend_beside(2, built[2])
    attend_beside(3, built[3])
    weights(2, [dot(lg_s[...], x)])
    direct_send(2)
    partial_grad = dot(lg_s[...].astype(F32).T.astype(BF), lw_s[...], 1, 1)
    own_t = own_s[...].T
    across_send(0)
    across_send(1)
    back_down.wait()
    back_up.wait()
    value_grad = own_t + back_s[0].astype(F32) + back_s[1].astype(F32)
    input_grad = dot(value_grad.astype(BF), vwt_s[...]) + partial_grad
    ig_ref[...] = input_grad.astype(BF)
    across_send(2)
    share_send(0)
    share_send(1)
    share_send(2)
    relay_send(0)
    share_all_bulk(1).wait_recv()
    share_all_bulk(2).wait_recv()
    relay(0, 1 - core).wait_recv()
    for n in range(3):
        settle(n)


def finish_kernel(
    aga_ref, agb_ref, agc_ref, ig_in, ig_hbm, gv_hbm, gl_hbm, go_hbm, gv_s, gl_s, go_s, sem
):
    copies = [
        pltpu.make_async_copy(src, dst, sem.at[n])
        for n, (src, dst) in enumerate(
            [
                (ig_in, ig_hbm),
                (go_s, go_hbm),
                (gv_s.at[:128], gv_hbm.at[:128]),
                (gv_s.at[128:], gv_hbm.at[128:]),
                (gl_s, gl_hbm),
            ]
        )
    ]
    copies[0].start()
    parts = [
        (
            aga_ref[c].reshape(CHUNKS[0], 128).astype(F32),
            agb_ref[c * 16 : c * 16 + 16].reshape(CHUNKS[1], 128).astype(F32),
        )
        for c in range(2)
    ]
    for c, (a, b) in enumerate(parts):
        cols = slice(c * 128, (c + 1) * 128)
        go_s[:128, cols] = a[128:]
        go_s[128:, cols] = b[128:]
    copies[1].start()
    for c, (a, b) in enumerate(parts):
        cols = slice(c * 128, (c + 1) * 128)
        gv_s[cols, :128] = a[:128].T
        gv_s[cols, 128:] = b[:128].T
        copies[2 + c].start()
    for c in range(2):
        cols = slice(c * 128, (c + 1) * 128)
        gl_s[cols, :] = agc_ref[c * 16 : c * 16 + 16].reshape(CHUNKS[2], 128).astype(F32).T
    copies[4].start()
    for copy in copies:
        copy.wait()


def body(features, corner_rows, corner_weights, out_grad, vw, lw, ow):
    vm = pl.BlockSpec(memory_space=pltpu.VMEM)
    hbm = pl.BlockSpec(memory_space=pltpu.HBM)
    dma = pltpu.SemaphoreType.DMA
    ig, aga, agb, agc = pl.pallas_call(
        whole_kernel,
        out_shape=(
            pltpu.VMEM((CELLS, D), BF),
            pltpu.VMEM((2, 16, CHUNKS[0] // 16, 128), BF),
            pltpu.VMEM((32, CHUNKS[1] // 16, 128), BF),
            pltpu.VMEM((32, CHUNKS[2] // 16, 128), BF),
        ),
        in_specs=[hbm] * 7,
        out_specs=[vm] * 4,
        scratch_shapes=[
            pltpu.VMEM((CELLS, D), BF),
            pltpu.VMEM((CELLS, D), BF),
            pltpu.VMEM((D, D), BF),
            pltpu.VMEM((D, HEADS * PTS), BF),
            pltpu.VMEM((D, D), BF),
            pltpu.VMEM((HEADS, 64, CELLS), I32),
            pltpu.VMEM((HEADS, 64, CELLS), F32),
            pltpu.VMEM((D, D), BF),
            pltpu.VMEM((2, CELLS, D), BF),
            pltpu.VMEM((3, D, D), BF),
            pltpu.VMEM((HEADS, PTS, CELLS), F32),
            pltpu.VMEM((D, CELLS), F32),
            pltpu.VMEM((D, CELLS), BF),
            pltpu.VMEM((12, 64, 128), F32),
            pltpu.VMEM((D, CELLS), F32),
            pltpu.VMEM((3, D, CELLS), BF),
            pltpu.VMEM((2, 3, 4, 64, 128), F32),
            pltpu.VMEM((PAIRS, 3, PAD, LANES), BF),
            pltpu.VMEM((HEADS * PTS, CELLS), BF),
            pltpu.VMEM((2, CELLS, D), BF),
            pltpu.VMEM((2, CELLS, D), BF),
            pltpu.VMEM((PAIRS, 2 * HEAD, LANES), BF),
            pltpu.VMEM((PAIRS, 3, 128, 2 * HEAD), BF),
            pltpu.VMEM((PAIRS, 2 * HEAD, LANES), F32),
            pltpu.VMEM((PAIRS, 3, 128, 128), I32),
            pltpu.VMEM((PAIRS, 3, 128, 128), F32),
            pltpu.VMEM((D, 128), BF),
            [pltpu.VMEM((2, n, 128), F32) for n in CHUNKS],
            [pltpu.VMEM((n, 128), BF) for n in CHUNKS[:1]],
            [pltpu.VMEM((n, 128), BF) for n in CHUNKS[:1]],
            [pltpu.VMEM((16, n // 16, 128), BF) for n in CHUNKS[:1]]
            + [pltpu.VMEM((32, n // 16, 128), BF) for n in CHUNKS[1:]],
            [pltpu.VMEM((16, n // 16, 128), BF) for n in CHUNKS[:1]]
            + [pltpu.VMEM((32, n // 16, 128), BF) for n in CHUNKS[1:]],
            [pltpu.VMEM((4, n // 16, 128), F32) for n in CHUNKS],
            dma((9,)),
            dma((4,)),
            dma((4,)),
            dma((1, 2)),
            dma((3,)),
            dma((3,)),
            dma((3,)),
            dma((3,)),
            dma((3,)),
            dma((3,)),
            dma((1,)),
            dma((1,)),
        ],
        compiler_params=pltpu.CompilerParams(
            collective_id=0, has_side_effects=True, vmem_limit_bytes=60 * 10**6
        ),
        name="whole",
    )(
        features[0].T,
        corner_rows[0],
        corner_weights[0],
        out_grad[0].T,
        vw,
        lw,
        ow,
    )
    ig, gv, gl, go = pl.pallas_call(
        finish_kernel,
        out_shape=(
            jax.ShapeDtypeStruct((CELLS, D), BF),
            jax.ShapeDtypeStruct((D, D), F32),
            jax.ShapeDtypeStruct((D, HEADS * PTS), F32),
            jax.ShapeDtypeStruct((D, D), F32),
        ),
        in_specs=[vm] * 4,
        out_specs=[hbm] * 4,
        scratch_shapes=[
            pltpu.VMEM((D, D), F32),
            pltpu.VMEM((D, HEADS * PTS), F32),
            pltpu.VMEM((D, D), F32),
            dma((5,)),
        ],
        compiler_params=pltpu.CompilerParams(vmem_limit_bytes=8 * 2**20),
        name="finish",
    )(aga, agb, agc, ig)
    return (ig.T[None], gv, gl, go)


def solution(mesh):
    placed = (
        P("dp", None, "band"),
        P("dp", None, None, "band"),
        P("dp", None, None, "band"),
        P("dp", None, "band"),
        P(),
        P(),
        P(),
    )
    return jax.shard_map(
        body,
        mesh=mesh,
        in_specs=placed,
        out_specs=(P("dp", None, "band"), P(), P(), P()),
        check_vma=False,
    )
```

```python
import jax
import jax.numpy as jnp
from jax import lax
from jax.experimental import pallas as pl
from jax.experimental.pallas import tpu as pltpu
from jax.sharding import PartitionSpec as P

HEADS = 8
LEVELS = 4
POINTS = 4
D = 256
CELLS = 172
PAD = 176
TAIL = CELLS - 128
GAP = 128 - 2 * TAIL
LANES = 384
PAIRS = HEADS // 2
SIDE = 4
HEAD = D // HEADS
PTS = LEVELS * POINTS
CHUNKS = (256, 256, 128)
BF = jnp.bfloat16
F32 = jnp.float32
I32 = jnp.int32


def dot(a, b, ca=1, cb=0):
    return lax.dot_general(a, b, (((ca,), (cb,)), ((), ())), preferred_element_type=F32)


def lane_pick(table, index):
    numbers = lax.GatherDimensionNumbers(
        offset_dims=(),
        collapsed_slice_dims=(1,),
        start_index_map=(1,),
        operand_batching_dims=(0,),
        start_indices_batching_dims=(0,),
    )
    return lax.gather(
        table,
        index[..., None],
        numbers,
        slice_sizes=(1, 1),
        mode=lax.GatherScatterMode.PROMISE_IN_BOUNDS,
    )


def whole_kernel(
    x_hbm,
    rows_hbm,
    cw_hbm,
    og_hbm,
    vw_hbm,
    lw_hbm,
    ow_hbm,
    ig_ref,
    aga_ref,
    agb_ref,
    agc_ref,
    x_s,
    og_s,
    vw_s,
    lw_s,
    ow_s,
    rows_s,
    cw_s,
    vwt_s,
    halo_s,
    v_s,
    att_s,
    g_s,
    samp_s,
    rep_s,
    own_s,
    vg_s,
    wide_s,
    m_s,
    lg_s,
    send_s,
    back_s,
    gp_s,
    gt_s,
    half_s,
    at_s,
    pick_s,
    rest_s,
    w_s,
    ps_s,
    pr_s,
    yr_s,
    in_sem,
    halo_sem,
    back_sem,
    ps_sem,
    pr_sem,
    ys_sem,
    yr_sem,
    as_sem,
    ar_sem,
    rs_sem,
    rr_sem,
):
    ag_refs = (aga_ref, agb_ref, agc_ref)
    band = lax.axis_index("band")
    image = lax.axis_index("dp")
    bands = lax.axis_size("band")
    images = lax.axis_size("dp")
    chips = bands // 2
    core = lax.rem(band, 2)
    chip = lax.div(band, 2)
    up = {"band": lax.rem(band + 1, bands)}
    down = {"band": lax.rem(band + bands - 1, bands)}
    partner = {"band": band + 1 - 2 * core}

    row, column = lax.div(chip, SIDE), lax.rem(chip, SIDE)
    steps = [(a, b) for a in range(SIDE) for b in range(SIDE)]
    steps.sort(key=lambda ab: -sum(min(n, SIDE - n) for n in ab))

    def peer(t):
        a, b = steps[t - 1]
        return lax.rem(row + a, SIDE) * SIDE + lax.rem(column + b, SIDE)

    def side(t):
        return core if t % 2 and t + 1 < bands else 1 - core

    def any_peer(t):
        return 2 * peer((t + 1) // 2) + side(t)

    def remote(src, dst, send, recv, where):
        return pltpu.make_async_remote_copy(
            src_ref=src,
            dst_ref=dst,
            send_sem=send,
            recv_sem=recv,
            device_id=where,
            device_id_type=pl.DeviceIdType.MESH,
        )

    def each(low, high, step):
        for t in range(low, high):
            step(t)

    barrier = pltpu.get_barrier_semaphore()

    def greet(where):
        pl.semaphore_signal(barrier, inc=1, device_id=where, device_id_type=pl.DeviceIdType.MESH)

    first, rest = pl.ds(0, 2), pl.ds(2, HEADS - 2)
    loads = [
        pltpu.make_async_copy(src, dst, in_sem.at[n])
        for n, (src, dst) in enumerate(
            [
                (x_hbm, x_s),
                (lw_hbm, lw_s),
                (rows_hbm.at[first], rows_s.at[first]),
                (cw_hbm.at[first], cw_s.at[first]),
                (vw_hbm, vw_s),
                (og_hbm, og_s),
                (ow_hbm, ow_s),
                (rows_hbm.at[rest], rows_s.at[rest]),
                (cw_hbm.at[rest], cw_s.at[rest]),
            ]
        )
    ]
    for load in loads:
        load.start()
    each(1, bands, lambda t: greet({"band": any_peer(t)}))
    each(1, images, lambda t: greet({"dp": lax.rem(image + t, images)}))

    loads[0].wait()
    loads[1].wait()
    x = x_s[...]
    att_s[...] = dot(lw_s[...].T, x, 1, 1).reshape(HEADS, PTS, CELLS)
    loads[2].wait()
    loads[3].wait()

    def packed(first, second):
        tail = jnp.concatenate(
            [first[:, 128:], second[:, 128:], jnp.zeros((first.shape[0], GAP), first.dtype)],
            axis=1,
        )
        return [first[:, :128], second[:, :128], tail]

    sub = lax.broadcasted_iota(I32, (16, 128), 0)
    ids = [(sub + cb * 16).astype(F32).astype(BF) for cb in range(11)]
    base = (band - 1) * CELLS
    nil = jnp.zeros((), BF)

    def build(i):
        cells = packed(rows_s[2 * i] - base, rows_s[2 * i + 1] - base)
        cw = packed(cw_s[2 * i], cw_s[2 * i + 1])
        logit = packed(att_s[2 * i], att_s[2 * i + 1])
        att = []
        for g in range(3):
            e = jnp.exp(logit[g])
            att.append(e / jnp.sum(e, axis=0, keepdims=True))
            rep = rep_s.at[(i % 2) * 6 + g]
            for c in range(4):
                rep[pl.ds(c, PTS, stride=4), :] = att[g]
            over1 = cells[g] >= CELLS
            over2 = cells[g] >= 2 * CELLS
            r = cells[g] - jnp.where(over2, 2 * CELLS, jnp.where(over1, CELLS, 0))
            w = (rep[...] * cw[g]).astype(BF).astype(F32)
            zero = jnp.zeros_like(w)
            wide = wide_s.at[i % 2, g]
            wide[0] = r.astype(F32)
            wide[1] = jnp.where(over1, zero, w)
            wide[2] = jnp.where(over1, jnp.where(over2, zero, w), zero)
            wide[3] = jnp.where(over2, w, zero)
            for cbs, levels in ((range(8), (0,)), (range(8, 10), (1,)), (range(10, 11), (2, 3))):
                acc = [[None] * 3 for _ in cbs]
                for lev in levels:
                    for k in range(lev * 16, lev * 16 + 16):
                        row = [
                            jnp.broadcast_to(wide[n, pl.ds(k, 1), :], (16, 128)).astype(BF)
                            for n in range(4)
                        ]
                        for at, cb in enumerate(cbs):
                            hit = row[0] == ids[cb]
                            for j in range(3):
                                term = jnp.where(hit, row[1 + j], nil)
                                old = acc[at][j]
                                acc[at][j] = term if old is None else old + term
                for at, cb in enumerate(cbs):
                    for j in range(3):
                        m_s[i, j, cb * 16 : cb * 16 + 16, g * 128 : (g + 1) * 128] = acc[at][j]
        return cells, cw, att

    def heads_of(i):
        return slice(i * 2 * HEAD, (i + 1) * 2 * HEAD)

    def parts(at):
        over1 = at >= CELLS
        over2 = at >= 2 * CELLS
        r = at - jnp.where(over2, 2 * CELLS, jnp.where(over1, CELLS, 0))
        return over1, over2, r < 128, jnp.bitwise_and(r, 127)

    def spread_grad(i):
        g0 = g_s[i * 2 * HEAD : i * 2 * HEAD + HEAD, :]
        g1 = g_s[i * 2 * HEAD + HEAD : (i + 1) * 2 * HEAD, :]
        none = jnp.zeros((HEAD, 128), F32)
        top = [
            g0[:, :128],
            none,
            jnp.concatenate([g0[:, 128:], none[:, : 128 - TAIL]], axis=1),
        ]
        bottom = [
            none,
            g1[:, :128],
            jnp.concatenate([none[:, :TAIL], g1[:, 128:], none[:, : 128 - 2 * TAIL]], axis=1),
        ]
        for g in range(3):
            both = jnp.concatenate([top[g], bottom[g]], axis=0)
            gp_s[i, :, g * 128 : (g + 1) * 128] = both.astype(BF)
            gt_s[i, g] = both.T.astype(BF)

    def project_own(i):
        hs = heads_of(i)
        half_s[i] = dot(v_s[1, hs, :CELLS], m_s[i, 1, :CELLS, :])
        for j in range(3):
            part = dot(gp_s[i], m_s[i, j, :CELLS, :], 1, 1)
            if j == 1:
                own_s[hs, :] = part
            vg_s[j, hs, :] = part.astype(BF)

    def project_beside(i):
        hs = heads_of(i)
        samp = half_s[i]
        for j in (0, 2):
            samp = samp + dot(v_s[j, hs, :CELLS], m_s[i, j, :CELLS, :])
        s0 = jnp.concatenate([samp[:HEAD, :128], samp[:HEAD, 256 : 256 + TAIL]], axis=1)
        s1 = jnp.concatenate(
            [samp[HEAD:, 128:256], samp[HEAD:, 256 + TAIL : 256 + 2 * TAIL]], axis=1
        )
        samp_s[hs, :] = jnp.concatenate([s0, s1], axis=0).astype(BF)

    def lookup(table, near, index):
        near_part = lane_pick(table[:, :128], index)
        return jnp.where(near, near_part, lane_pick(table[:, 128:], index))

    def groups(g):
        return range(0, 128 if g < 2 else 2 * TAIL, 8)

    def attend_own(i, built):
        for g in range(3):
            at = jnp.concatenate([built[0][g], jnp.zeros((64, 128), I32)], axis=0).T
            at_s[i, g] = at
            score = dot(gt_s[i, g], v_s[1, heads_of(i), :])
            for q in groups(g):
                _, _, near, index = parts(at[q : q + 8])
                pick_s[i, g, q : q + 8, :] = lookup(score[q : q + 8], near, index)

    def attend_beside(i, built):
        _, cw, att = built
        lgs = []
        for g in range(3):
            below = dot(gt_s[i, g], v_s[0, heads_of(i), :128])
            above = dot(gt_s[i, g], v_s[2, heads_of(i), :128])
            rest = dot(gt_s[i, g], rest_s[heads_of(i), :])
            for q in groups(g):
                qs = slice(q, q + 8)
                over1, over2, near, index = parts(at_s[i, g, qs, :])
                index = jnp.where(near, index, jnp.where(over2, index + TAIL, index))
                pick = jnp.where(over2, lane_pick(above[qs], index), lane_pick(below[qs], index))
                pick = jnp.where(near, pick, lane_pick(rest[qs], index))
                mine = jnp.where(over2, pick, pick_s[i, g, qs, :])
                pick_s[i, g, qs, :] = jnp.where(over1, mine, pick)
            rep = rep_s.at[(i % 2) * 6 + 3 + g]
            rep[...] = pick_s[i, g, :, :64].T * cw[g]
            ag = jnp.zeros((PTS, 128), F32)
            for c in range(4):
                ag = ag + rep[pl.ds(c, PTS, stride=4), :]
            lgs.append(att[g] * (ag - jnp.sum(att[g] * ag, axis=0, keepdims=True)))
        l0 = jnp.concatenate([lgs[0], lgs[2][:, :TAIL]], axis=1)
        l1 = jnp.concatenate([lgs[1], lgs[2][:, TAIL : 2 * TAIL]], axis=1)
        lg_s[i * 2 * PTS : (i + 1) * 2 * PTS, :] = jnp.concatenate([l0, l1], axis=0).astype(BF)

    scale = 1.0 / float(images * bands * CELLS) ** 0.5

    def weights(n, blocks):
        for c in range(2):
            at = 0
            for block in blocks:
                w_s[n][c, at : at + block.shape[0], :] = block[:, c * 128 : (c + 1) * 128]
                at += block.shape[0]

    def pair_weights(n, pairs):
        first, last = pairs[0] * 2 * HEAD, (pairs[-1] + 1) * 2 * HEAD
        gv = dot(vg_s[0, first:last, :], halo_s[0])
        gv = gv + dot(vg_s[1, first:last, :], x)
        gv = gv + dot(vg_s[2, first:last, :], halo_s[1])
        weights(n, [gv, dot(samp_s[first:last, :], og)])

    def across(n, t):
        q = lax.rem(image + t, images)
        spot = yr_s[n].at[image]
        return remote(spot, spot, ys_sem.at[n], yr_sem.at[n], {"dp": q})

    def across_bulk(n):
        some = yr_s[n].at[pl.ds(0, 3)]
        return remote(some, some, ys_sem.at[n], yr_sem.at[n], partner)

    slot = core * 16 + chip

    def direct(n, t):
        q = any_peer(t)
        return remote(
            ps_s[n].at[side(t) * 16 + peer((t + 1) // 2)],
            pr_s[n].at[slot],
            ps_sem.at[n],
            pr_sem.at[n],
            {"band": q},
        )

    def direct_bulk(n):
        some = pl.ds(0, 31)
        return remote(
            ps_s[n].at[some], pr_s[n].at[some], ps_sem.at[n], pr_sem.at[n], partner
        )

    def direct_send(n):
        ps_s[n][...] = w_s[n][...].astype(BF).reshape(ps_s[n].shape)
        each(1, bands, lambda t: direct(n, t).start())
        pr_s[n][slot] = ps_s[n][slot]

    def across_send(n):
        direct_bulk(n).wait_recv()
        pieces = [pr_s[n][q] for q in range(32)]
        sums = [piece.astype(F32) for piece in pieces]
        while len(sums) > 1:
            sums = [a + b for a, b in zip(sums[::2], sums[1::2])]
        yr_s[n][image] = sums[0]
        each(0, images - 1, lambda t: across(n, (2, 1, 3)[t]).start())

    def share(n, t):
        q = peer(t)
        spot = ag_refs[n].at[core, chip]
        return remote(spot, spot, as_sem.at[n], ar_sem.at[n], {"band": 2 * q + core})

    def share_bulk(n):
        some = ag_refs[n].at[core, pl.ds(0, 15)]
        return remote(some, some, as_sem.at[n], ar_sem.at[n], partner)

    def share_all(n, t):
        spot = ag_refs[n].at[slot]
        where = {"band": any_peer(t)}
        return remote(spot, spot, as_sem.at[n], ar_sem.at[n], where)

    def share_all_bulk(n):
        some = ag_refs[n].at[pl.ds(0, 31)]
        return remote(some, some, as_sem.at[n], ar_sem.at[n], partner)

    def share_send(n):
        across_bulk(n).wait_recv()
        total = yr_s[n][0]
        for q in range(1, images):
            total = total + yr_s[n][q]
        total = (total * scale).astype(BF)
        if n < 1:
            ag_refs[n][core, chip] = total
            each(1, chips, lambda t: share(n, t).start())
        else:
            ag_refs[n][slot] = total
            each(1, bands, lambda t: share_all(n, t).start())

    def relay(n, side):
        spot = ag_refs[n].at[side]
        return remote(spot, spot, rs_sem.at[n], rr_sem.at[n], partner)

    def relay_send(n):
        share_bulk(n).wait_recv()
        relay(n, core).start()

    def settle(n):
        across_bulk(n).wait_send()
        direct_bulk(n).wait_send()
        if n < 1:
            share_bulk(n).wait_send()
            relay(n, core).wait_send()
        else:
            share_all_bulk(n).wait_send()

    def widen(v):
        return jnp.concatenate([v, jnp.zeros((D, D - CELLS), F32)], axis=1).astype(BF)

    def own(i):
        spread_grad(i)
        project_own(i)
        attend_own(i, built[i])

    built = [build(0)]
    for load in loads[4:]:
        load.wait()
    vwt_s[...] = vw_s[...].T
    og = og_s[...]
    g_s[...] = dot(ow_s[...], og, 1, 1).astype(BF).astype(F32)
    v_s[1] = widen(dot(vwt_s[...], x, 1, 1))
    for i in range(PAIRS):
        pick_s[i, 2, 2 * TAIL :, :] = jnp.zeros((128 - 2 * TAIL, 128), F32)
    built.append(build(1))
    own(0)

    pl.semaphore_wait(barrier, bands - 1 + images - 1)
    halo_up = remote(x_s, halo_s.at[0], halo_sem.at[0], halo_sem.at[2], up)
    halo_down = remote(x_s, halo_s.at[1], halo_sem.at[1], halo_sem.at[3], down)
    halo_up.start()
    halo_down.start()

    built.append(build(2))
    own(1)
    built.append(build(3))
    own(2)
    own(3)

    send_s[0] = vg_s[0].T
    send_s[1] = vg_s[2].T
    back_down = remote(send_s.at[0], back_s.at[1], back_sem.at[0], back_sem.at[2], down)
    back_up = remote(send_s.at[1], back_s.at[0], back_sem.at[1], back_sem.at[3], up)
    back_down.start()
    back_up.start()
    halo_up.wait()
    halo_down.wait()

    low = dot(vwt_s[...], halo_s[0], 1, 1)
    high = dot(vwt_s[...], halo_s[1], 1, 1)
    v_s[0] = widen(low)
    v_s[2] = widen(high)
    rest_s[...] = jnp.concatenate(
        [low[:, 128:], high[:, 128:], jnp.zeros((D, GAP), F32)], axis=1
    ).astype(BF)
    for i in range(PAIRS):
        project_beside(i)
    pair_weights(0, (0, 1))
    direct_send(0)
    pair_weights(1, (2, 3))
    direct_send(1)
    attend_beside(0, built[0])
    attend_beside(1, built[1])
    attend_beside(2, built[2])
    attend_beside(3, built[3])
    weights(2, [dot(lg_s[...], x)])
    direct_send(2)
    partial_grad = dot(lg_s[...].astype(F32).T.astype(BF), lw_s[...], 1, 1)
    own_t = own_s[...].T
    across_send(0)
    across_send(1)
    back_down.wait()
    back_up.wait()
    value_grad = own_t + back_s[0].astype(F32) + back_s[1].astype(F32)
    input_grad = dot(value_grad.astype(BF), vwt_s[...]) + partial_grad
    ig_ref[...] = input_grad.astype(BF)
    across_send(2)
    share_send(0)
    share_send(1)
    share_send(2)
    relay_send(0)
    share_all_bulk(1).wait_recv()
    share_all_bulk(2).wait_recv()
    relay(0, 1 - core).wait_recv()
    for n in range(3):
        settle(n)


def finish_kernel(
    aga_ref, agb_ref, agc_ref, ig_in, ig_hbm, gv_hbm, gl_hbm, go_hbm, gv_s, gl_s, go_s, sem
):
    copies = [
        pltpu.make_async_copy(src, dst, sem.at[n])
        for n, (src, dst) in enumerate(
            [
                (ig_in, ig_hbm),
                (go_s, go_hbm),
                (gv_s.at[:128], gv_hbm.at[:128]),
                (gv_s.at[128:], gv_hbm.at[128:]),
                (gl_s, gl_hbm),
            ]
        )
    ]
    copies[0].start()
    parts = [
        (
            aga_ref[c].reshape(CHUNKS[0], 128).astype(F32),
            agb_ref[c * 16 : c * 16 + 16].reshape(CHUNKS[1], 128).astype(F32),
        )
        for c in range(2)
    ]
    for c, (a, b) in enumerate(parts):
        cols = slice(c * 128, (c + 1) * 128)
        go_s[:128, cols] = a[128:]
        go_s[128:, cols] = b[128:]
    copies[1].start()
    for c, (a, b) in enumerate(parts):
        cols = slice(c * 128, (c + 1) * 128)
        gv_s[cols, :128] = a[:128].T
        gv_s[cols, 128:] = b[:128].T
        copies[2 + c].start()
    for c in range(2):
        cols = slice(c * 128, (c + 1) * 128)
        gl_s[cols, :] = agc_ref[c * 16 : c * 16 + 16].reshape(CHUNKS[2], 128).astype(F32).T
    copies[4].start()
    for copy in copies:
        copy.wait()


def body(features, corner_rows, corner_weights, out_grad, vw, lw, ow):
    vm = pl.BlockSpec(memory_space=pltpu.VMEM)
    hbm = pl.BlockSpec(memory_space=pltpu.HBM)
    dma = pltpu.SemaphoreType.DMA
    ig, aga, agb, agc = pl.pallas_call(
        whole_kernel,
        out_shape=(
            pltpu.VMEM((CELLS, D), BF),
            pltpu.VMEM((2, 16, CHUNKS[0] // 16, 128), BF),
            pltpu.VMEM((32, CHUNKS[1] // 16, 128), BF),
            pltpu.VMEM((32, CHUNKS[2] // 16, 128), BF),
        ),
        in_specs=[hbm] * 7,
        out_specs=[vm] * 4,
        scratch_shapes=[
            pltpu.VMEM((CELLS, D), BF),
            pltpu.VMEM((CELLS, D), BF),
            pltpu.VMEM((D, D), BF),
            pltpu.VMEM((D, HEADS * PTS), BF),
            pltpu.VMEM((D, D), BF),
            pltpu.VMEM((HEADS, 64, CELLS), I32),
            pltpu.VMEM((HEADS, 64, CELLS), F32),
            pltpu.VMEM((D, D), BF),
            pltpu.VMEM((2, CELLS, D), BF),
            pltpu.VMEM((3, D, D), BF),
            pltpu.VMEM((HEADS, PTS, CELLS), F32),
            pltpu.VMEM((D, CELLS), F32),
            pltpu.VMEM((D, CELLS), BF),
            pltpu.VMEM((12, 64, 128), F32),
            pltpu.VMEM((D, CELLS), F32),
            pltpu.VMEM((3, D, CELLS), BF),
            pltpu.VMEM((2, 3, 4, 64, 128), F32),
            pltpu.VMEM((PAIRS, 3, PAD, LANES), BF),
            pltpu.VMEM((HEADS * PTS, CELLS), BF),
            pltpu.VMEM((2, CELLS, D), BF),
            pltpu.VMEM((2, CELLS, D), BF),
            pltpu.VMEM((PAIRS, 2 * HEAD, LANES), BF),
            pltpu.VMEM((PAIRS, 3, 128, 2 * HEAD), BF),
            pltpu.VMEM((PAIRS, 2 * HEAD, LANES), F32),
            pltpu.VMEM((PAIRS, 3, 128, 128), I32),
            pltpu.VMEM((PAIRS, 3, 128, 128), F32),
            pltpu.VMEM((D, 128), BF),
            [pltpu.VMEM((2, n, 128), F32) for n in CHUNKS],
            [pltpu.VMEM((32, n // 16, 128), BF) for n in CHUNKS],
            [pltpu.VMEM((32, n // 16, 128), BF) for n in CHUNKS],
            [pltpu.VMEM((4, n // 16, 128), F32) for n in CHUNKS],
            dma((9,)),
            dma((4,)),
            dma((4,)),
            dma((3,)),
            dma((3,)),
            dma((3,)),
            dma((3,)),
            dma((3,)),
            dma((3,)),
            dma((1,)),
            dma((1,)),
        ],
        compiler_params=pltpu.CompilerParams(
            collective_id=0, has_side_effects=True, vmem_limit_bytes=60 * 10**6
        ),
        name="whole",
    )(
        features[0].T,
        corner_rows[0],
        corner_weights[0],
        out_grad[0].T,
        vw,
        lw,
        ow,
    )
    ig, gv, gl, go = pl.pallas_call(
        finish_kernel,
        out_shape=(
            jax.ShapeDtypeStruct((CELLS, D), BF),
            jax.ShapeDtypeStruct((D, D), F32),
            jax.ShapeDtypeStruct((D, HEADS * PTS), F32),
            jax.ShapeDtypeStruct((D, D), F32),
        ),
        in_specs=[vm] * 4,
        out_specs=[hbm] * 4,
        scratch_shapes=[
            pltpu.VMEM((D, D), F32),
            pltpu.VMEM((D, HEADS * PTS), F32),
            pltpu.VMEM((D, D), F32),
            dma((5,)),
        ],
        compiler_params=pltpu.CompilerParams(vmem_limit_bytes=8 * 2**20),
        name="finish",
    )(aga, agb, agc, ig)
    return (ig.T[None], gv, gl, go)


def solution(mesh):
    placed = (
        P("dp", None, "band"),
        P("dp", None, None, "band"),
        P("dp", None, None, "band"),
        P("dp", None, "band"),
        P(),
        P(),
        P(),
    )
    return jax.shard_map(
        body,
        mesh=mesh,
        in_specs=placed,
        out_specs=(P("dp", None, "band"), P(), P(), P()),
        check_vma=False,
    )
```
